512 devices in a mesh: dp: 16 (over x_lo, y), expert: 32 (over x_hi, z, core).
Axes of the slice: x: 4 (x_hi: 2, x_lo: 2; x = x_hi * 2 + x_lo), y: 8, z: 8, core: 2. Of those that a mesh axis runs over, the one named last changes fastest.
Arguments:
- tokens: bfloat16 [65536, 3584], P(('dp', 'expert')), may hold values from -6 to 6
- grad_out: bfloat16 [65536, 3584], P(('dp', 'expert')), may hold values from -1.5 to 1.5
- route: int32 [16, 32, 32, 1], P('dp', 'expert'), may hold values from 0 to 127
- gates: bfloat16 [16, 32, 32, 1], P('dp', 'expert'), may hold values from 0.099609375 to 1
- w_gate: bfloat16 [32, 3584, 768], P('expert', 'dp'), may hold values from -0.09375 to 0.09375
- w_up: bfloat16 [32, 3584, 768], P('expert', 'dp'), may hold values from -0.09375 to 0.09375
- w_down: bfloat16 [32, 768, 3584], P('expert', None, 'dp'), may hold values from -0.21875 to 0.21875
Outputs:
- grad_tokens: bfloat16 [65536, 3584], P(('dp', 'expert'))
- grad_w_gate: bfloat16 [32, 3584, 768], P('expert', 'dp')
- grad_w_up: bfloat16 [32, 3584, 768], P('expert', 'dp')
- grad_w_down: bfloat16 [32, 768, 3584], P('expert', None, 'dp')
- grad_gates: float32 [16, 32, 32, 1], P('dp', 'expert')
The draws below stay inside these ranges and needn't reach their ends.
Inputs may be any that keep to these rules, and one draw needn't show every extreme that they name: route[i, j, e, s] is the position, among the 128 tokens of the device at dp index i and expert index j, of the token that expert e takes in slot s from that device; a token may be taken by several experts or slots.
All inputs are finite; a program needn't handle non-finite values.
Results may differ from the reference program's by a relative error of at most 0.017.
Values may be sent and summed in bfloat16 or wider, within the bound.
A program may use at most 64 MiB of HBM per device.

```python
import math
import jax
import jax.numpy as jnp
from jax import lax

D = 3584
H = 768
SLOT = 1
TOK_DEV = 128
EXPERTS = 32
TOKENS = 65536
N_DP = 16
N_EXPERT = 32


def touch_ends(values, own_key, low, top_value):
    place = [jax.random.randint(jax.random.fold_in(own_key, axis), (), 0, length) for axis, length in enumerate(values.shape)]
    main_axis = values.shape.index(max(values.shape))
    next_to = place[:main_axis] + [(place[main_axis] + 1) % values.shape[main_axis]] + place[main_axis + 1:]
    return values.at[tuple(place)].set(low).at[tuple(next_to)].set(top_value)


def steps_of(stream_key, shape, cuts, least, top_value):
    def one(position, parts):
        draws = jax.random.uniform(jax.random.fold_in(jax.random.fold_in(stream_key, 6), position), (parts,), jnp.float32, least / len(cuts), top_value / len(cuts))
        return jnp.repeat(jnp.exp(draws), shape[position] // parts).reshape((-1,) + (1,) * (len(shape) - position - 1))

    level = one(*cuts[0])
    for cut in cuts[1:]:
        level = level * one(*cut)
    return level


def gaussian(own_key, dims, width, reach, split=(), kind=jnp.bfloat16):
    values = jax.random.normal(own_key, dims, jnp.float32) * width
    if len(split) > 0:
        values = steps_of(own_key, dims, split, -0.22, 0.18) * values
    return jnp.clip(values, min=-reach, max=reach).astype(kind)


def setup_inputs(seed: int = 0) -> dict:
    arg_keys = jax.random.split(jax.random.key(seed), 8)
    return {
        "tokens": gaussian(arg_keys[0], (TOKENS, D), 1.0, 6.0, ((0, 512),)),
        "grad_out": gaussian(arg_keys[1], (TOKENS, D), 0.25, 1.5, ((0, 512),)),
        "route": touch_ends(jax.random.randint(arg_keys[2], (N_DP, N_EXPERT, EXPERTS, SLOT), 0, TOK_DEV), jax.random.fold_in(arg_keys[2], 1), 0, TOK_DEV - 1).astype(jnp.int32),
        "gates": jnp.clip(jnp.exp(math.log(1.0) - 2.306499 * jax.random.uniform(arg_keys[3], (N_DP, N_EXPERT, EXPERTS, SLOT), jnp.float32) ** steps_of(arg_keys[3], (N_DP, N_EXPERT, EXPERTS, SLOT), ((0, 16), (1, 32)), -0.2, 0.2)), 0.099609375, 1.0).astype(jnp.bfloat16),
        "w_gate": gaussian(arg_keys[4], (EXPERTS, D, H), D ** -0.5, 0.09375, ((0, 32), (1, 16))),
        "w_up": gaussian(arg_keys[5], (EXPERTS, D, H), D ** -0.5, 0.09375, ((0, 32), (1, 16))),
        "w_down": gaussian(arg_keys[6], (EXPERTS, H, D), H ** -0.5, 0.21875, ((0, 32), (2, 16))),
    }


def reference(tokens, grad_out, route, gates, w_gate, w_up, w_down):
    n_dp, n_ex, experts, slots = route.shape
    rows = n_dp * n_ex * slots
    offsets = (jnp.arange(n_dp * n_ex, dtype=jnp.int32) * TOK_DEV).reshape(n_dp, n_ex, 1, 1)
    chosen = jnp.transpose(route + offsets, (2, 0, 1, 3)).reshape(experts, rows).astype(jnp.int32)
    weights_of = jnp.transpose(gates, (2, 0, 1, 3)).reshape(experts, rows)

    def one_expert(args):
        picks, gate_w, wg, wu, wd = args
        x_rows = tokens[picks]
        dy_rows = grad_out[picks]
        gate_pre = jnp.dot(x_rows, wg, preferred_element_type=jnp.float32)
        up_pre = jnp.dot(x_rows, wu, preferred_element_type=jnp.float32)
        hidden = (jax.nn.silu(gate_pre) * up_pre).astype(jnp.bfloat16)
        out_rows = jnp.dot(hidden, wd, preferred_element_type=jnp.float32).astype(jnp.bfloat16)
        grad_gate = jnp.sum(dy_rows.astype(jnp.float32) * out_rows.astype(jnp.float32), axis=1)
        weighted = (gate_w.astype(jnp.float32)[:, None] * dy_rows.astype(jnp.float32)).astype(jnp.bfloat16)
        grad_hidden = jnp.dot(weighted, wd.T, preferred_element_type=jnp.float32)
        sig = jax.nn.sigmoid(gate_pre)
        grad_gate_pre = (grad_hidden * up_pre * sig * (1.0 + gate_pre * (1.0 - sig))).astype(jnp.bfloat16)
        grad_up_pre = (grad_hidden * gate_pre * sig).astype(jnp.bfloat16)
        grad_rows = (jnp.dot(grad_gate_pre, wg.T, preferred_element_type=jnp.float32)
                     + jnp.dot(grad_up_pre, wu.T, preferred_element_type=jnp.float32)).astype(jnp.bfloat16)
        grad_wg = jnp.dot(x_rows.T, grad_gate_pre, preferred_element_type=jnp.float32).astype(jnp.bfloat16)
        grad_wu = jnp.dot(x_rows.T, grad_up_pre, preferred_element_type=jnp.float32).astype(jnp.bfloat16)
        grad_wd = jnp.dot(hidden.T, weighted, preferred_element_type=jnp.float32).astype(jnp.bfloat16)
        return grad_gate, grad_rows, grad_wg, grad_wu, grad_wd

    grad_gate, grad_rows, grad_wg, grad_wu, grad_wd = lax.map(
        one_expert, (chosen, weights_of, w_gate, w_up, w_down))
    grad_tokens = jnp.zeros((TOKENS, D), jnp.float32).at[chosen.reshape(-1)].add(
        grad_rows.reshape(experts * rows, D).astype(jnp.float32)).astype(jnp.bfloat16)
    grad_gates = jnp.transpose(grad_gate.reshape(experts, n_dp, n_ex, slots), (1, 2, 0, 3))
    return grad_tokens, grad_wg, grad_wu, grad_wd, grad_gates
```

```python
import functools

import jax
import jax.numpy as jnp
from jax import lax
from jax.experimental import pallas as pl
from jax.experimental.pallas import tpu as pltpu
from jax.sharding import PartitionSpec as P

NX = 2
F32 = jnp.float32
BF16 = jnp.bfloat16


def dot(a, b, ca=1, cb=0):
    return lax.dot_general(a, b, (((ca,), (cb,)), ((), ())), preferred_element_type=F32)


def kernel(
    cfg,
    tokens, grad_out, route, gates, wg, wu, wd,
    gt_out, gwg_out, gwu_out, gwd_out, gg_out,
    tok_v, dyo_v, wg_v, wu_v, wd_v, wide, perm, a1, r1, a2, r2, part, acc, arm,
    xsend, xrecv, q_all, own_gg, a3, r3, a4, r4, gw_v, gwd_v, gt_v,
    load_sem, s1_sem, r1_sem, s2_sem, r2_sem, as_sem, ar_sem, xs_sem, xr_sem,
    qs_sem, qr_sem, qxs_sem, qxr_sem, s3_sem, r3_sem, s4_sem, r4_sem, out_sem,
):
    n_dp, n_ex, piece, width, hid = cfg
    ny = n_dp // NX
    n_rows = n_dp * n_ex
    d_model = n_dp * piece
    cap = n_ex
    half = 3 * hid // 2
    long_arm = ny // 2
    win = width + 128

    me = lax.axis_index("dp")
    ex = lax.axis_index("expert")
    xl = me // ny
    y = lax.rem(me, ny)
    pair = (1 - xl) * ny + y

    def y_of(off):
        return lax.rem(y + off + 2 * ny, ny)

    def rows(k, n):
        return pl.ds(pl.multiple_of(k * n, n), n)

    barrier = pltpu.get_barrier_semaphore()

    def greet_dp(s, c):
        pl.semaphore_signal(barrier, inc=1, device_id={"dp": lax.rem(me + s, n_dp)})
        return c

    def greet_ex(s, c):
        pl.semaphore_signal(barrier, inc=1, device_id={"expert": lax.rem(ex + s, n_ex)})
        return c

    lax.fori_loop(1, n_dp, greet_dp, 0)
    lax.fori_loop(1, n_ex, greet_ex, 0)

    loads = [
        pltpu.make_async_copy(src, dst, load_sem.at[n])
        for n, (src, dst) in enumerate(
            [(tokens, tok_v), (grad_out, dyo_v), (wg, wg_v), (wu, wu_v), (wd, wd_v)]
        )
    ]
    for load in loads:
        load.start()

    r_id = lax.broadcasted_iota(jnp.int32, (n_rows, n_rows), 0)
    c_id = lax.broadcasted_iota(jnp.int32, (n_rows, n_rows), 1)
    perm[...] = jnp.where(c_id == lax.rem(r_id, n_dp) * n_ex + r_id // n_dp, 1.0, 0.0).astype(BF16)

    tok_dev = tokens.shape[0]
    t_id = lax.broadcasted_iota(jnp.int32, (n_ex, tok_dev), 1)
    pick = jnp.where(t_id == route[...], 1.0, 0.0).astype(BF16)
    gate_own = gates[...].astype(F32)
    lane = lax.broadcasted_iota(jnp.int32, (n_ex, width), 1)

    wide[:, d_model:] = jnp.zeros((n_ex, wide.shape[1] - d_model), F32)

    def gather(q, src):
        wide[:, :d_model] = dot(pick, src[...])
        for d in range(n_dp):
            start = (piece * d) // 128 * 128
            shift = piece * d - start
            v = wide[:, start:start + win]
            if shift:
                v = pltpu.roll(v, win - shift, 1)
            v = v[:, :width]
            pad = jnp.where(lane == piece, gate_own, 0.0) if q == 0 else 0.0
            a1[q, d * n_ex:(d + 1) * n_ex, :] = jnp.where(lane < piece, v, pad).astype(BF16)

    def dp_copy(q, k, slot, src, dst, send, recv):
        return pltpu.make_async_remote_copy(
            src_ref=src.at[q, rows(k, n_ex)],
            dst_ref=dst.at[q, rows(slot, n_ex)],
            send_sem=send.at[q, k],
            recv_sem=recv.at[q, slot],
            device_id={"dp": k},
        )

    def ex_copy(q, k, slot, src, dst, send, recv):
        return pltpu.make_async_remote_copy(
            src_ref=src.at[q, rows(k, n_dp)],
            dst_ref=dst.at[q, rows(slot, n_dp)],
            send_sem=send.at[q, k],
            recv_sem=recv.at[q, slot],
            device_id={"expert": k},
        )

    def exchange(copy, n, mine, size, q, src, dst, send, recv):
        pltpu.make_async_copy(
            src.at[q, rows(mine, size)], dst.at[q, rows(mine, size)], recv.at[q, mine]
        ).start()

        def go(s, c):
            copy(q, lax.rem(mine + s, n), mine, src, dst, send, recv).start()
            return c

        lax.fori_loop(1, n, go, 0)

    def arrive(n, size, q, src, dst, recv):
        def one(k, c):
            pltpu.make_async_copy(
                src.at[q, rows(k, size)], dst.at[q, rows(k, size)], recv.at[q, k]
            ).wait()
            return c

        lax.fori_loop(0, n, one, 0)

    def drain(copy, n, mine, q, src, dst, send, recv):
        def one(s, c):
            copy(q, lax.rem(mine + s, n), mine, src, dst, send, recv).wait_send()
            return c

        lax.fori_loop(1, n, one, 0)

    loads[0].wait()
    gather(0, tok_v)
    pl.semaphore_wait(barrier, n_dp + n_ex - 2)
    exchange(dp_copy, n_dp, me, n_ex, 0, a1, r1, s1_sem, r1_sem)
    loads[1].wait()
    gather(1, dyo_v)
    exchange(dp_copy, n_dp, me, n_ex, 1, a1, r1, s1_sem, r1_sem)
    for q in range(2):
        arrive(n_dp, n_ex, q, a1, r1, r1_sem)
        a2[q] = dot(perm[...], r1[q]).astype(BF16)
        exchange(ex_copy, n_ex, ex, n_dp, q, a2, r2, s2_sem, r2_sem)
    for load in loads[2:]:
        load.wait()

    def partial(m, value):
        part[:, :, :, m * hid:(m + 1) * hid] = value.astype(BF16).reshape(NX, ny, cap, hid)

    arrive(n_ex, n_dp, 0, a2, r2, r2_sem)
    partial(0, dot(r2[0, :, :piece], wg_v[...]))
    partial(1, dot(r2[0, :, :piece], wu_v[...]))
    arrive(n_ex, n_dp, 1, a2, r2, r2_sem)
    partial(2, dot(r2[1, :, :piece], wd_v[...], 1, 1))

    def arm_len(g, s):
        return long_arm if g == s else long_arm - 1

    def cols(g):
        return slice(g * half, (g + 1) * half)

    def arm_copy(g, s, h):
        sign = 1 if s == 0 else -1
        n = arm_len(g, s)
        owner = y_of(sign * (n - h))
        src = part.at[:, owner, :, cols(g)] if h == 0 else acc.at[s, h, :, :, cols(g)]
        return pltpu.make_async_remote_copy(
            src_ref=src,
            dst_ref=arm.at[s, h, :, :, cols(g)],
            send_sem=as_sem.at[s, h, g],
            recv_sem=ar_sem.at[s, h, g],
            device_id={"dp": xl * ny + y_of(sign)},
        )

    lanes = [(g, s) for g in range(2) for s in range(2)]
    for h in range(long_arm):
        for g, s in lanes:
            sign = 1 if s == 0 else -1
            n = arm_len(g, s)
            if h >= n:
                continue
            if h > 0:
                arm_copy(g, s, h - 1).wait_recv()
                mine = part[:, y_of(sign * (n - h)), :, cols(g)].astype(F32)
                got = arm[s, h - 1, :, :, cols(g)].astype(F32)
                acc[s, h, :, :, cols(g)] = (mine + got).astype(BF16)
            arm_copy(g, s, h).start()

    def total(side, g):
        out = part[side, y, :, cols(g)].astype(F32)
        for s in range(2):
            out = out + arm[s, arm_len(g, s) - 1, side, :, cols(g)].astype(F32)
        return out

    def x_copy(g):
        return pltpu.make_async_remote_copy(
            src_ref=xsend.at[:, cols(g)],
            dst_ref=xrecv.at[:, cols(g)],
            send_sem=xs_sem.at[g],
            recv_sem=xr_sem.at[g],
            device_id={"dp": pair},
        )

    for g in range(2):
        for s in range(2):
            arm_copy(g, s, arm_len(g, s) - 1).wait_recv()
        xsend[:, cols(g)] = total(1 - xl, g).astype(BF16)
        x_copy(g).start()
    pieces = []
    for g in range(2):
        x_copy(g).wait_recv()
        pieces.append(total(xl, g) + xrecv[:, cols(g)].astype(F32))
    full = jnp.concatenate(pieces, axis=1)
    gate_pre = full[:, :hid]
    up_pre = full[:, hid:2 * hid]
    base = full[:, 2 * hid:]
    gate_rows = r2[0, rows(me, cap), :].astype(F32)
    wl = lax.broadcasted_iota(jnp.int32, (cap, width), 1)
    gate_w = jnp.sum(jnp.where(wl == piece, gate_rows, 0.0), axis=1, keepdims=True)
    sig = 1.0 / (1.0 + jnp.exp(-gate_pre))
    act = gate_pre * sig
    hidden = act * up_pre
    grad_hidden = gate_w * base
    own_gg[...] = jnp.broadcast_to(
        jnp.sum(hidden * base, axis=1, keepdims=True), own_gg.shape
    )
    mine = q_all.at[xl, y]
    mine[:, :hid] = (gate_w * hidden).astype(BF16)
    mine[:, hid:2 * hid] = (
        grad_hidden * up_pre * sig * (1.0 + gate_pre * (1.0 - sig))
    ).astype(BF16)
    mine[:, 2 * hid:] = (grad_hidden * act).astype(BF16)

    def q_pair():
        return pltpu.make_async_remote_copy(
            src_ref=q_all.at[xl, y],
            dst_ref=q_all.at[xl, y],
            send_sem=qxs_sem.at[0],
            recv_sem=qxr_sem.at[0],
            device_id={"dp": pair},
        )

    def q_copy(c, s, h):
        sign = 1 if s == 0 else -1
        side = xl if c == 0 else 1 - xl
        block = q_all.at[side, y_of(-sign * h)]
        if h == long_arm - 1:
            block = block.at[:, cols(s)]
        return pltpu.make_async_remote_copy(
            src_ref=block,
            dst_ref=block,
            send_sem=qs_sem.at[c, s, h],
            recv_sem=qr_sem.at[c, s, h],
            device_id={"dp": xl * ny + y_of(sign)},
        )

    q_pair().start()
    for h in range(long_arm):
        for c in range(2):
            if h == 0 and c == 1:
                q_pair().wait_recv()
            for s in range(2):
                if h > 0:
                    q_copy(c, s, h - 1).wait_recv()
                q_copy(c, s, h).start()
    for c in range(2):
        for s in range(2):
            q_copy(c, s, long_arm - 1).wait_recv()

    def back(m):
        return q_all[:, :, :, m * hid:(m + 1) * hid].reshape(n_rows, hid)

    a3[0, :, width - 128:] = jnp.zeros((n_rows, 128), BF16)
    a3[0, :, :piece] = (dot(back(1), wg_v[...], 1, 1) + dot(back(2), wu_v[...], 1, 1)).astype(BF16)
    tail = a3[0, rows(me, cap), width - 128:].astype(F32)
    tl = lax.broadcasted_iota(jnp.int32, tail.shape, 1) + (width - 128)
    rest = own_gg[...]
    for n in range(3):
        top = rest.astype(BF16).astype(F32)
        tail = jnp.where(tl == piece + n, top, tail)
        rest = rest - top
    a3[0, rows(me, cap), width - 128:] = tail.astype(BF16)
    exchange(ex_copy, n_ex, ex, n_dp, 0, a3, r3, s3_sem, r3_sem)

    outs = [
        pltpu.make_async_copy(gw_v.at[0], gwg_out, out_sem.at[0]),
        pltpu.make_async_copy(gw_v.at[1], gwu_out, out_sem.at[1]),
        pltpu.make_async_copy(gwd_v, gwd_out, out_sem.at[2]),
        pltpu.make_async_copy(gt_v, gt_out, out_sem.at[3]),
    ]
    gw_v[0] = dot(r2[0, :, :piece], back(1), 0, 0).astype(BF16)
    outs[0].start()
    gw_v[1] = dot(r2[0, :, :piece], back(2), 0, 0).astype(BF16)
    outs[1].start()
    gwd_v[...] = dot(back(0), r2[1, :, :piece], 0, 0).astype(BF16)
    outs[2].start()

    arrive(n_ex, n_dp, 0, a3, r3, r3_sem)
    a4[0] = dot(perm[...], r3[0], 0, 0).astype(BF16)
    exchange(dp_copy, n_dp, me, n_ex, 0, a4, r4, s4_sem, r4_sem)
    wide[...] = jnp.zeros(wide.shape, F32)
    arrive(n_dp, n_ex, 0, a4, r4, r4_sem)
    sums = jnp.zeros((n_ex, width), F32)
    for d in range(n_dp):
        start = (piece * d) // 128 * 128
        shift = piece * d - start
        v = r4[0, d * n_ex:(d + 1) * n_ex, :].astype(F32)
        sums = sums + jnp.where((lane >= piece) & (lane < piece + 3), v, 0.0)
        v = jnp.concatenate([jnp.where(lane < piece, v, 0.0), jnp.zeros((n_ex, 128), F32)], axis=1)
        if shift:
            v = pltpu.roll(v, shift, 1)
        wide[:, start:start + win] += v
    gg_out[...] = jnp.sum(sums, axis=1, keepdims=True)
    gt_v[...] = dot(pick, wide[:, :d_model].astype(BF16), 0, 0).astype(BF16)
    outs[3].start()

    for q in range(2):
        drain(dp_copy, n_dp, me, q, a1, r1, s1_sem, r1_sem)
        drain(ex_copy, n_ex, ex, q, a2, r2, s2_sem, r2_sem)
    for g, s in lanes:
        for h in range(arm_len(g, s)):
            arm_copy(g, s, h).wait_send()
    for g in range(2):
        x_copy(g).wait_send()
    q_pair().wait_send()
    for h in range(long_arm):
        for c in range(2):
            for s in range(2):
                q_copy(c, s, h).wait_send()
    drain(ex_copy, n_ex, ex, 0, a3, r3, s3_sem, r3_sem)
    drain(dp_copy, n_dp, me, 0, a4, r4, s4_sem, r4_sem)
    for out in outs:
        out.wait()


def local(tokens, grad_out, route, gates, w_gate, w_up, w_down):
    n_dp = lax.axis_size("dp")
    n_ex = lax.axis_size("expert")
    piece, hid = w_gate.shape[1:]
    tok_dev, d_model = tokens.shape
    width = (piece + 3 + 127) // 128 * 128
    n_rows = n_dp * n_ex
    ny = n_dp // NX
    arm_n = ny // 2
    cap = n_ex
    dma = pltpu.SemaphoreType.DMA
    any_spec = pl.BlockSpec(memory_space=pl.ANY)
    vmem_spec = pl.BlockSpec(memory_space=pltpu.VMEM)
    outs = pl.pallas_call(
        functools.partial(kernel, (n_dp, n_ex, piece, width, hid)),
        out_shape=(
            jax.ShapeDtypeStruct((tok_dev, d_model), BF16),
            jax.ShapeDtypeStruct((piece, hid), BF16),
            jax.ShapeDtypeStruct((piece, hid), BF16),
            jax.ShapeDtypeStruct((hid, piece), BF16),
            jax.ShapeDtypeStruct((n_ex, 1), F32),
        ),
        in_specs=[any_spec, any_spec, vmem_spec, vmem_spec, any_spec, any_spec, any_spec],
        out_specs=(any_spec, any_spec, any_spec, any_spec, vmem_spec),
        scratch_shapes=[
            pltpu.VMEM((tok_dev, d_model), BF16),
            pltpu.VMEM((tok_dev, d_model), BF16),
            pltpu.VMEM((piece, hid), BF16),
            pltpu.VMEM((piece, hid), BF16),
            pltpu.VMEM((hid, piece), BF16),
            pltpu.VMEM((n_ex, d_model + width + 128), F32),
            pltpu.VMEM((n_rows, n_rows), BF16),
            pltpu.VMEM((2, n_rows, width), BF16),
            pltpu.VMEM((2, n_rows, width), BF16),
            pltpu.VMEM((2, n_rows, width), BF16),
            pltpu.VMEM((2, n_rows, width), BF16),
            pltpu.VMEM((NX, ny, cap, 3 * hid), BF16),
            pltpu.VMEM((2, arm_n, NX, cap, 3 * hid), BF16),
            pltpu.VMEM((2, arm_n, NX, cap, 3 * hid), BF16),
            pltpu.VMEM((cap, 3 * hid), BF16),
            pltpu.VMEM((cap, 3 * hid), BF16),
            pltpu.VMEM((NX, ny, cap, 3 * hid), BF16),
            pltpu.VMEM((cap, 128), F32),
            pltpu.VMEM((1, n_rows, width), BF16),
            pltpu.VMEM((1, n_rows, width), BF16),
            pltpu.VMEM((1, n_rows, width), BF16),
            pltpu.VMEM((1, n_rows, width), BF16),
            pltpu.VMEM((2, piece, hid), BF16),
            pltpu.VMEM((hid, piece), BF16),
            pltpu.VMEM((tok_dev, d_model), BF16),
            dma((5,)),
            dma((2, n_dp)), dma((2, n_dp)),
            dma((2, n_ex)), dma((2, n_ex)),
            dma((2, arm_n, 2)), dma((2, arm_n, 2)),
            dma((2,)), dma((2,)),
            dma((2, 2, arm_n)), dma((2, 2, arm_n)),
            dma((1,)), dma((1,)),
            dma((1, n_ex)), dma((1, n_ex)),
            dma((1, n_dp)), dma((1, n_dp)),
            dma((4,)),
        ],
        compiler_params=pltpu.CompilerParams(
            collective_id=0, has_side_effects=True, vmem_limit_bytes=56 * 1024 * 1024
        ),
        name="moe",
    )(
        tokens,
        grad_out,
        route.reshape(n_ex, 1),
        gates.reshape(n_ex, 1),
        w_gate[0],
        w_up[0],
        w_down[0],
    )
    gt, gwg, gwu, gwd, gg = outs
    return gt, gwg[None], gwu[None], gwd[None], gg.reshape(gates.shape)


def solution(mesh):
    return jax.shard_map(
        local,
        mesh=mesh,
        in_specs=(
            P(("dp", "expert"), None),
            P(("dp", "expert"), None),
            P("dp", "expert", None, None),
            P("dp", "expert", None, None),
            P("expert", "dp", None),
            P("expert", "dp", None),
            P("expert", None, "dp"),
        ),
        out_specs=(
            P(("dp", "expert"), None),
            P("expert", "dp", None),
            P("expert", "dp", None),
            P("expert", None, "dp"),
            P("dp", "expert", None, None),
        ),
        check_vma=False,
    )
```

```python
import functools

import jax
import jax.numpy as jnp
from jax import lax
from jax.experimental import pallas as pl
from jax.experimental.pallas import tpu as pltpu
from jax.sharding import PartitionSpec as P

NX = 2
F32 = jnp.float32
BF16 = jnp.bfloat16


def dot(a, b, ca=1, cb=0):
    return lax.dot_general(a, b, (((ca,), (cb,)), ((), ())), preferred_element_type=F32)


def one_hot_rows(route, tok_dev):
    n_ex = route.shape[1]
    t_id = lax.broadcasted_iota(jnp.int32, (tok_dev, n_ex), 0)
    return jnp.where(t_id == jnp.broadcast_to(route, (tok_dev, n_ex)), 1.0, 0.0).astype(BF16)


def kernel(
    cfg,
    tokens, grad_out, route, gates, wg, wu, wd,
    r4, gwg_out, gwu_out, gwd_out,
    tok_v, dyo_v, wg_v, wu_v, wd_v, route_v, gates_v, wide, perm, a1, r1, a2, r2,
    part, xa, arm_a, acc_a, arm_b, acc_b, xsend, xrecv, q_all, own_gg, a3, r3, a4, gw_v,
    load_sem, s1_sem, r1_sem, s2_sem, r2_sem, xas_sem, xar_sem, as_sem, ar_sem, xs_sem, xr_sem,
    qs_sem, qr_sem, qxs_sem, qxr_sem, s3_sem, r3_sem, s4_sem, r4_sem, out_sem,
):
    n_dp, n_ex, piece, width, hid = cfg
    ny = n_dp // NX
    n_rows = n_dp * n_ex
    d_model = n_dp * piece
    cap = n_ex
    hh = hid // 2
    win = width + 128

    me = lax.axis_index("dp")
    ex = lax.axis_index("expert")
    xl = me // ny
    y = lax.rem(me, ny)
    pair = (1 - xl) * ny + y

    def y_of(off):
        return lax.rem(y + off + 2 * ny, ny)

    def y_dev(off):
        return {"dp": xl * ny + y_of(off)}

    def rows(k, n):
        return pl.ds(pl.multiple_of(k * n, n), n)

    barrier = pltpu.get_barrier_semaphore()

    def greet_dp(s, c):
        pl.semaphore_signal(barrier, inc=1, device_id={"dp": lax.rem(me + s, n_dp)})
        return c

    def greet_ex(s, c):
        pl.semaphore_signal(barrier, inc=1, device_id={"expert": lax.rem(ex + s, n_ex)})
        return c

    lax.fori_loop(1, n_ex, greet_ex, 0)
    lax.fori_loop(1, n_dp, greet_dp, 0)

    loads = [
        pltpu.make_async_copy(src, dst, load_sem.at[n])
        for n, (src, dst) in enumerate(
            [
                (route, route_v), (gates, gates_v), (tokens, tok_v), (grad_out, dyo_v),
                (wg, wg_v), (wu, wu_v), (wd, wd_v),
            ]
        )
    ]
    for load in loads:
        load.start()

    lane = lax.broadcasted_iota(jnp.int32, (n_ex, width), 1)
    wide[:, d_model:] = jnp.zeros((n_ex, wide.shape[1] - d_model), F32)
    for load in loads[:3]:
        load.wait()
    pick = one_hot_rows(route_v[...], tok_v.shape[0])
    e_row = lax.broadcasted_iota(jnp.int32, (n_ex, n_ex), 0)
    e_col = lax.broadcasted_iota(jnp.int32, (n_ex, n_ex), 1)
    gate_row = jnp.broadcast_to(gates_v[...].astype(F32), (n_ex, n_ex))
    gate_own = jnp.sum(jnp.where(e_row == e_col, gate_row, 0.0), axis=1, keepdims=True)

    def gather(q, src):
        wide[:, :d_model] = dot(pick, src[...], 0, 0)
        for d in range(n_dp):
            start = (piece * d) // 128 * 128
            shift = piece * d - start
            v = wide[:, start:start + win]
            if shift:
                v = pltpu.roll(v, win - shift, 1)
            v = v[:, :width]
            pad = jnp.where(lane == piece, gate_own, 0.0) if q == 0 else 0.0
            a1[q, d * n_ex:(d + 1) * n_ex, :] = jnp.where(lane < piece, v, pad).astype(BF16)

    class Exchange:
        def __init__(self, axis, q, src, dst, send, recv):
            self.axis = axis
            self.n, self.mine, self.size = (n_dp, me, n_ex) if axis == "dp" else (n_ex, ex, n_dp)
            self.src, self.dst = src.at[q], dst.at[q]
            self.send, self.recv = send.at[q], recv.at[q]

        def start(self):
            own = rows(self.mine, self.size)
            pltpu.make_async_copy(self.src.at[own], self.dst.at[own], self.recv).start()

            def go(s, c):
                k = lax.rem(self.mine + s, self.n)
                pltpu.make_async_remote_copy(
                    src_ref=self.src.at[rows(k, self.size)],
                    dst_ref=self.dst.at[own],
                    send_sem=self.send,
                    recv_sem=self.recv,
                    device_id={self.axis: k},
                ).start()
                return c

            lax.fori_loop(1, self.n, go, 0)

        def arrive(self):
            pltpu.make_async_copy(self.src, self.dst, self.recv).wait()

        def drain(self):
            sent = self.src.at[pl.ds(0, (self.n - 1) * self.size)]
            pltpu.make_async_copy(sent, sent, self.send).wait()

    ex1 = [Exchange("dp", q, a1, r1, s1_sem, r1_sem) for q in range(2)]
    ex2 = [Exchange("expert", q, a2, r2, s2_sem, r2_sem) for q in range(2)]
    ex3 = Exchange("expert", 0, a3, r3, s3_sem, r3_sem)
    ex4 = Exchange("dp", 0, a4, r4, s4_sem, r4_sem)

    gather(0, tok_v)
    pl.semaphore_wait(barrier, n_dp + n_ex - 2)
    ex1[0].start()
    loads[3].wait()
    gather(1, dyo_v)
    ex1[1].start()
    r_id = lax.broadcasted_iota(jnp.int32, (n_rows, n_rows), 0)
    c_id = lax.broadcasted_iota(jnp.int32, (n_rows, n_rows), 1)
    perm[...] = jnp.where(c_id == lax.rem(r_id, n_dp) * n_ex + r_id // n_dp, 1.0, 0.0).astype(BF16)
    for q in range(2):
        ex1[q].arrive()
        a2[q] = dot(perm[...], r1[q]).astype(BF16)
        ex2[q].start()
    for load in loads[4:]:
        load.wait()

    def partial(m, value):
        value = value.astype(BF16)
        for c in range(2):
            part[m, c] = value[:, c * hh:(c + 1) * hh].reshape(NX, ny, cap, hh)

    def arm_len(m, c, s):
        return ny // 2 - (m + c + s) % 2

    def sign(s):
        return 1 - 2 * s

    def xa_copy(m, off):
        block = y_of(off)
        return pltpu.make_async_remote_copy(
            src_ref=part.at[m, 0, 1 - xl, block],
            dst_ref=xa.at[m, block],
            send_sem=xas_sem.at[0],
            recv_sem=xar_sem.at[m, off % ny],
            device_id={"dp": pair},
        )

    far_first = sorted(range(-(ny // 2) + 1, ny // 2 + 1), key=lambda o: -abs(o))

    def xa_send(m):
        for off in far_first:
            xa_copy(m, off).start()

    def arm_copy(m, c, s, h):
        arm, acc = ((arm_a, acc_a), (arm_b, acc_b))[c]
        if c == 1 and h == 0:
            src = part.at[m, 1, :, y_of(sign(s) * arm_len(m, c, s))]
        else:
            src = acc.at[m, s, h]
        return pltpu.make_async_remote_copy(
            src_ref=src,
            dst_ref=arm.at[m, s, h],
            send_sem=as_sem.at[c],
            recv_sem=ar_sem.at[m, c, s, h],
            device_id=y_dev(sign(s)),
        )

    def hop(m, c, h):
        for s in range(2):
            n = arm_len(m, c, s)
            if h >= n:
                continue
            off = sign(s) * (n - h)
            owner = y_of(off)
            if c == 0:
                xa_copy(m, off).wait_recv()
                v = part[m, 0, xl, owner].astype(F32) + xa[m, owner].astype(F32)
                if h > 0:
                    arm_copy(m, c, s, h - 1).wait_recv()
                    v = v + arm_a[m, s, h - 1].astype(F32)
                acc_a[m, s, h] = v.astype(BF16)
            elif h > 0:
                arm_copy(m, c, s, h - 1).wait_recv()
                v = part[m, 1, :, owner].astype(F32) + arm_b[m, s, h - 1].astype(F32)
                acc_b[m, s, h] = v.astype(BF16)
            arm_copy(m, c, s, h).start()

    def x_copy(m):
        return pltpu.make_async_remote_copy(
            src_ref=xsend.at[m],
            dst_ref=xrecv.at[m],
            send_sem=xs_sem.at[0],
            recv_sem=xr_sem.at[m],
            device_id={"dp": pair},
        )

    def b_total(m, side):
        v = part[m, 1, side, y].astype(F32)
        for s in range(2):
            v = v + arm_b[m, s, arm_len(m, 1, s) - 1, side].astype(F32)
        return v

    def b_end(m):
        for s in range(2):
            arm_copy(m, 1, s, arm_len(m, 1, s) - 1).wait_recv()
        xsend[m] = b_total(m, 1 - xl).astype(BF16)
        x_copy(m).start()

    def finish(m):
        xa_copy(m, 0).wait_recv()
        v = part[m, 0, xl, y].astype(F32) + xa[m, y].astype(F32)
        for s in range(2):
            n = arm_len(m, 0, s)
            arm_copy(m, 0, s, n - 1).wait_recv()
            v = v + arm_a[m, s, n - 1].astype(F32)
        x_copy(m).wait_recv()
        return jnp.concatenate([v, b_total(m, xl) + xrecv[m].astype(F32)], axis=1)

    last = ny // 2

    ex2[0].arrive()
    partial(0, dot(r2[0, :, :piece], wg_v[...]))
    xa_send(0)
    hop(0, 1, 0)
    partial(1, dot(r2[0, :, :piece], wu_v[...]))
    xa_send(1)
    hop(1, 1, 0)
    hop(0, 0, 0)
    hop(0, 1, 1)
    ex2[1].arrive()
    partial(2, dot(r2[1, :, :piece], wd_v[...]))
    xa_send(2)
    hop(2, 1, 0)
    for h in range(1, last + 2):
        for m, c, k in (
            (1, 1, h), (1, 0, h - 1), (0, 0, h), (0, 1, h + 1), (2, 1, h), (2, 0, h - 1)
        ):
            if k < last:
                hop(m, c, k)
            elif k == last and c == 1:
                b_end(m)
    gate_pre = finish(0)
    up_pre = finish(1)
    gate_rows = r2[0, rows(me, cap), :].astype(F32)
    wl = lax.broadcasted_iota(jnp.int32, (cap, width), 1)
    gate_w = jnp.sum(jnp.where(wl == piece, gate_rows, 0.0), axis=1, keepdims=True)
    sig = 1.0 / (1.0 + jnp.exp(-gate_pre))
    act = gate_pre * sig
    hidden = act * up_pre
    slope = up_pre * sig * (1.0 + gate_pre * (1.0 - sig))
    base = finish(2)
    grad_hidden = gate_w * base

    def keep(m, value):
        value = value.astype(BF16)
        for c in range(2):
            q_all[m, c, xl, y] = value[:, c * hh:(c + 1) * hh]

    def q_remote(block, send, recv, device):
        return pltpu.make_async_remote_copy(
            src_ref=block, dst_ref=block, send_sem=send, recv_sem=recv, device_id=device
        )

    def q_xb(m):
        return q_remote(q_all.at[m, 1, xl, y], qxs_sem.at[1], qxr_sem.at[m, 1], {"dp": pair})

    def q_xa(m, off):
        block = q_all.at[m, 0, xl, y_of(off)]
        return q_remote(block, qxs_sem.at[0], qxr_sem.at[m, 0], {"dp": pair})

    def q_arm(m, c, s, h):
        owner = y_of(-sign(s) * h)
        block = q_all.at[m, 0, xl, owner] if c == 0 else q_all.at[m, 1, :, owner]
        return q_remote(block, qs_sem.at[c], qr_sem.at[m, c, s, h], y_dev(sign(s)))

    def q_hop(m, c, h):
        if h == 0:
            if c == 0:
                q_xa(m, 0).start()
            else:
                q_xb(m).wait_recv()
        for s in range(2):
            n = arm_len(m, c, s)
            if h > n:
                continue
            if h > 0:
                q_arm(m, c, s, h - 1).wait_recv()
            if h < n:
                q_arm(m, c, s, h).start()
            if c == 0 and h > 0:
                q_xa(m, -sign(s) * h).start()

    def q_end(m):
        side = q_all.at[m, 0, 1 - xl]
        pltpu.make_async_copy(side, side, qxr_sem.at[m, 0]).wait()

    keep(1, grad_hidden * slope)
    q_xb(1).start()
    q_hop(1, 0, 0)
    keep(2, grad_hidden * act)
    q_xb(2).start()
    q_hop(2, 0, 0)
    keep(0, gate_w * hidden)
    q_xb(0).start()
    own_gg[...] = jnp.broadcast_to(jnp.sum(hidden * base, axis=1, keepdims=True), own_gg.shape)
    q_hop(1, 1, 0)
    q_hop(2, 1, 0)
    q_hop(0, 0, 0)
    for h in range(1, last + 1):
        q_hop(1, 0, h)
        q_hop(1, 1, h)
        q_hop(2, 0, h)
        q_hop(2, 1, h)
        q_hop(0, 1, h - 1)
        if h < last:
            q_hop(0, 0, h)
    q_end(1)
    q_end(2)

    def back(m):
        return jnp.concatenate(
            [q_all[m, c].reshape(n_rows, hh) for c in range(2)], axis=1
        )

    a3[0, :, width - 128:] = jnp.zeros((n_rows, 128), BF16)
    a3[0, :, :piece] = (dot(back(1), wg_v[...], 1, 1) + dot(back(2), wu_v[...], 1, 1)).astype(BF16)
    tail = a3[0, rows(me, cap), width - 128:].astype(F32)
    tl = lax.broadcasted_iota(jnp.int32, tail.shape, 1) + (width - 128)
    rest = own_gg[...]
    for n in range(3):
        top = rest.astype(BF16).astype(F32)
        tail = jnp.where(tl == piece + n, top, tail)
        rest = rest - top
    a3[0, rows(me, cap), width - 128:] = tail.astype(BF16)
    ex3.start()

    q_hop(0, 0, last)
    q_hop(0, 1, last)
    outs = [
        pltpu.make_async_copy(gw_v.at[m], dst, out_sem.at[m])
        for m, dst in ((1, gwg_out), (2, gwu_out), (0, gwd_out))
    ]
    gw_v[1] = dot(r2[0, :, :piece], back(1), 0, 0).astype(BF16)
    outs[0].start()
    gw_v[2] = dot(r2[0, :, :piece], back(2), 0, 0).astype(BF16)
    outs[1].start()

    ex3.arrive()
    a4[0] = dot(perm[...], r3[0], 0, 0).astype(BF16)
    ex4.start()
    q_end(0)
    gw_v[0] = dot(r2[1, :, :piece], back(0), 0, 0).astype(BF16)
    outs[2].start()
    ex4.arrive()

    for x in (*ex1, *ex2, ex3, ex4):
        x.drain()

    def sent(ref, sem):
        pltpu.make_async_copy(ref, ref, sem).wait()

    sent(part.at[:, 0, 0], xas_sem.at[0])
    sent(part.at[:, 0, 0, pl.ds(0, ny - 1)], as_sem.at[0])
    sent(part.at[:, 1, :, pl.ds(0, ny - 1)], as_sem.at[1])
    sent(xsend, xs_sem.at[0])
    sent(part.at[:, 0, 0], qxs_sem.at[0])
    sent(xsend, qxs_sem.at[1])
    sent(part.at[:, 0, 0, pl.ds(0, ny - 1)], qs_sem.at[0])
    sent(part.at[:, 1, :, pl.ds(0, ny - 1)], qs_sem.at[1])
    for out in outs:
        out.wait()


def last_kernel(
    cfg, r4, route, gwg, gwu, gwd, gt_out, gg_out, gwg_out, gwu_out, gwd_out,
    r4_v, route_v, gw_v, wide, gt_v, gg_v, in_sem, out_sem,
):
    n_dp, n_ex, piece, width, hid = cfg
    d_model = n_dp * piece
    win = width + 128
    ins = [
        pltpu.make_async_copy(src, dst, in_sem.at[n])
        for n, (src, dst) in enumerate(
            [(r4, r4_v), (route, route_v)]
            + [(src, gw_v.at[m]) for m, src in enumerate((gwg, gwu, gwd))]
        )
    ]
    outs = [
        pltpu.make_async_copy(src, dst, out_sem.at[n])
        for n, (src, dst) in enumerate(
            [(gw_v.at[m], dst) for m, dst in enumerate((gwg_out, gwu_out, gwd_out))]
            + [(gg_v, gg_out), (gt_v, gt_out)]
        )
    ]
    for copy in ins:
        copy.start()
    wide[...] = jnp.zeros(wide.shape, F32)
    ins[0].wait()
    ins[1].wait()
    lane = lax.broadcasted_iota(jnp.int32, (n_ex, width), 1)
    sums = jnp.zeros((n_ex, width), F32)
    for d in range(n_dp):
        start = (piece * d) // 128 * 128
        shift = piece * d - start
        v = r4_v[0, d * n_ex:(d + 1) * n_ex, :].astype(F32)
        sums = sums + jnp.where((lane >= piece) & (lane < piece + 3), v, 0.0)
        v = jnp.concatenate([jnp.where(lane < piece, v, 0.0), jnp.zeros((n_ex, 128), F32)], axis=1)
        if shift:
            v = pltpu.roll(v, shift, 1)
        wide[:, start:start + win] += v
    for n in range(3):
        ins[2 + n].wait()
        outs[n].start()
    e_row = lax.broadcasted_iota(jnp.int32, (n_ex, n_ex), 0)
    e_col = lax.broadcasted_iota(jnp.int32, (n_ex, n_ex), 1)
    column = jnp.broadcast_to(jnp.sum(sums, axis=1, keepdims=True), (n_ex, n_ex))
    gg_v[...] = jnp.sum(jnp.where(e_row == e_col, column, 0.0), axis=0, keepdims=True)
    outs[3].start()
    pick = one_hot_rows(route_v[...], gt_v.shape[0])
    gt_v[...] = dot(pick, wide[:, :d_model].astype(BF16)).astype(BF16)
    outs[4].start()
    for copy in outs:
        copy.wait()


def local(tokens, grad_out, route, gates, w_gate, w_up, w_down):
    n_dp = lax.axis_size("dp")
    n_ex = lax.axis_size("expert")
    piece, hid = w_gate.shape[1:]
    tok_dev, d_model = tokens.shape
    width = (piece + 3 + 127) // 128 * 128
    n_rows = n_dp * n_ex
    ny = n_dp // NX
    hops = ny // 2
    cap = n_ex
    hh = hid // 2
    dma = pltpu.SemaphoreType.DMA
    any_spec = pl.BlockSpec(memory_space=pl.ANY)
    cfg = (n_dp, n_ex, piece, width, hid)
    weights = jax.ShapeDtypeStruct((piece, hid), BF16)
    route_row = route.reshape(1, n_ex)
    wide = pltpu.VMEM((n_ex, d_model + width + 128), F32)
    block = pltpu.VMEM((2, n_rows, width), BF16)
    one_block = pltpu.VMEM((1, n_rows, width), BF16)
    r4, gwg, gwu, gwd = pl.pallas_call(
        functools.partial(kernel, cfg),
        out_shape=(jax.ShapeDtypeStruct((1, n_rows, width), BF16), weights, weights, weights),
        in_specs=[any_spec] * 7,
        out_specs=(any_spec,) * 4,
        scratch_shapes=[
            pltpu.VMEM((tok_dev, d_model), BF16),
            pltpu.VMEM((tok_dev, d_model), BF16),
            pltpu.VMEM((piece, hid), BF16),
            pltpu.VMEM((piece, hid), BF16),
            pltpu.VMEM((piece, hid), BF16),
            pltpu.VMEM((1, n_ex), jnp.int32),
            pltpu.VMEM((1, n_ex), BF16),
            wide,
            pltpu.VMEM((n_rows, n_rows), BF16),
            block, block, block, block,
            pltpu.VMEM((3, 2, NX, ny, cap, hh), BF16),
            pltpu.VMEM((3, ny, cap, hh), BF16),
            pltpu.VMEM((3, 2, hops, cap, hh), BF16),
            pltpu.VMEM((3, 2, hops, cap, hh), BF16),
            pltpu.VMEM((3, 2, hops, NX, cap, hh), BF16),
            pltpu.VMEM((3, 2, hops, NX, cap, hh), BF16),
            pltpu.VMEM((3, cap, hh), BF16),
            pltpu.VMEM((3, cap, hh), BF16),
            pltpu.VMEM((3, 2, NX, ny, cap, hh), BF16),
            pltpu.VMEM((cap, 128), F32),
            one_block, one_block, one_block,
            pltpu.VMEM((3, piece, hid), BF16),
            dma((7,)),
            dma((2,)), dma((2,)),
            dma((2,)), dma((2,)),
            dma((1,)), dma((3, ny)),
            dma((2,)), dma((3, 2, 2, hops)),
            dma((1,)), dma((3,)),
            dma((2,)), dma((3, 2, 2, hops)),
            dma((2,)), dma((3, 2)),
            dma((1,)), dma((1,)),
            dma((1,)), dma((1,)),
            dma((3,)),
        ],
        compiler_params=pltpu.CompilerParams(
            collective_id=0, has_side_effects=True, vmem_limit_bytes=56 * 1024 * 1024
        ),
        name="moe",
    )(
        tokens,
        grad_out,
        route_row,
        gates.reshape(1, n_ex),
        w_gate[0],
        w_up[0],
        jnp.swapaxes(w_down[0], 0, 1),
    )
    gt, gg, gwg, gwu, gwd = pl.pallas_call(
        functools.partial(last_kernel, cfg),
        out_shape=(
            jax.ShapeDtypeStruct((tok_dev, d_model), BF16),
            jax.ShapeDtypeStruct((1, n_ex), F32),
            weights, weights, weights,
        ),
        in_specs=[any_spec] * 5,
        out_specs=(any_spec,) * 5,
        scratch_shapes=[
            pltpu.VMEM((1, n_rows, width), BF16),
            pltpu.VMEM((1, n_ex), jnp.int32),
            pltpu.VMEM((3, piece, hid), BF16),
            wide,
            pltpu.VMEM((tok_dev, d_model), BF16),
            pltpu.VMEM((1, n_ex), F32),
            dma((5,)),
            dma((5,)),
        ],
        compiler_params=pltpu.CompilerParams(vmem_limit_bytes=56 * 1024 * 1024),
        name="scatter",
    )(r4, route_row, gwg, gwu, gwd)
    return (
        gt, gwg[None], gwu[None], jnp.swapaxes(gwd, 0, 1)[None], gg.reshape(gates.shape),
    )


def solution(mesh):
    return jax.shard_map(
        local,
        mesh=mesh,
        in_specs=(
            P(("dp", "expert"), None),
            P(("dp", "expert"), None),
            P("dp", "expert", None, None),
            P("dp", "expert", None, None),
            P("expert", "dp", None),
            P("expert", "dp", None),
            P("expert", None, "dp"),
        ),
        out_specs=(
            P(("dp", "expert"), None),
            P("expert", "dp", None),
            P("expert", "dp", None),
            P("expert", None, "dp"),
            P("dp", "expert", None, None),
        ),
        check_vma=False,
    )
```

```python
import functools

import jax
import jax.numpy as jnp
from jax import lax
from jax.experimental import pallas as pl
from jax.experimental.pallas import tpu as pltpu
from jax.sharding import PartitionSpec as P

NX = 2
F32 = jnp.float32
BF16 = jnp.bfloat16


def dot(a, b, ca=1, cb=0):
    return lax.dot_general(a, b, (((ca,), (cb,)), ((), ())), preferred_element_type=F32)


def one_hot_rows(route, tok_dev):
    n_ex = route.shape[1]
    t_id = lax.broadcasted_iota(jnp.int32, (tok_dev, n_ex), 0)
    return jnp.where(t_id == jnp.broadcast_to(route, (tok_dev, n_ex)), 1.0, 0.0).astype(BF16)


def kernel(
    cfg,
    tokens, grad_out, route, gates, wg, wu, wd,
    r4, gwg_out, gwu_out, gwd_out,
    tok_v, dyo_v, wg_v, wu_v, wd_v, route_v, gates_v, wide, perm, a1, b1, r1, a2, r2, xd,
    part, xa, arm_a, acc_a, arm_b, acc_b, xsend, xrecv, q_all, own_gg, grad_rows, a3, r3, a4, gw_v,
    load_sem, s1_sem, r1_sem, s2_sem, r2_sem, xas_sem, xar_sem, as_sem, ar_sem, xs_sem, xr_sem,
    qs_sem, qr_sem, qxs_sem, qxr_sem, s3_sem, r3_sem, s4_sem, r4_sem, out_sem,
):
    n_dp, n_ex, piece, width, hid = cfg
    ny = n_dp // NX
    n_rows = n_dp * n_ex
    d_model = n_dp * piece
    cap = n_ex
    hh = hid // 2
    win = width + 128
    lanes = width // 2

    me = lax.axis_index("dp")
    ex = lax.axis_index("expert")
    xl = me // ny
    y = lax.rem(me, ny)
    pair = (1 - xl) * ny + y

    def y_of(off):
        return lax.rem(y + off + 2 * ny, ny)

    def y_dev(off):
        return {"dp": xl * ny + y_of(off)}

    def rows(k, n):
        return pl.ds(pl.multiple_of(k * n, n), n)

    barrier = pltpu.get_barrier_semaphore()

    def greet_dp(s, c):
        pl.semaphore_signal(barrier, inc=1, device_id={"dp": lax.rem(me + s, n_dp)})
        return c

    def greet_ex(s, c):
        pl.semaphore_signal(barrier, inc=1, device_id={"expert": lax.rem(ex + s, n_ex)})
        return c

    lax.fori_loop(1, n_ex, greet_ex, 0)
    lax.fori_loop(1, n_dp, greet_dp, 0)

    loads = [
        pltpu.make_async_copy(src, dst, load_sem.at[n])
        for n, (src, dst) in enumerate(
            [
                (route, route_v), (gates, gates_v), (tokens, tok_v), (grad_out, dyo_v),
                (wg, wg_v), (wu, wu_v), (wd, wd_v),
            ]
        )
    ]
    for load in loads:
        load.start()

    lane = lax.broadcasted_iota(jnp.int32, (n_ex, width), 1)
    wide[:, d_model:] = jnp.zeros((n_ex, wide.shape[1] - d_model), F32)
    for load in loads[:3]:
        load.wait()
    pick = one_hot_rows(route_v[...], tok_v.shape[0])
    e_row = lax.broadcasted_iota(jnp.int32, (n_ex, n_ex), 0)
    e_col = lax.broadcasted_iota(jnp.int32, (n_ex, n_ex), 1)
    gate_row = jnp.broadcast_to(gates_v[...].astype(F32), (n_ex, n_ex))
    gate_own = jnp.sum(jnp.where(e_row == e_col, gate_row, 0.0), axis=1, keepdims=True)

    def gather(q, src):
        wide[:, :d_model] = dot(pick, src[...], 0, 0)
        for d in range(n_dp):
            start = (piece * d) // 128 * 128
            shift = piece * d - start
            v = wide[:, start:start + win]
            if shift:
                v = pltpu.roll(v, win - shift, 1)
            v = v[:, :width]
            pad = jnp.where(lane == piece, gate_own, 0.0) if q == 0 else 0.0
            v = jnp.where(lane < piece, v, pad).astype(BF16)
            for c in range(2):
                a1[q, c, d * n_ex:(d + 1) * n_ex, :] = v[:, c * lanes:(c + 1) * lanes]

    class Exchange:
        def __init__(self, axis, q, c, src, dst, send, recv):
            self.axis = axis
            self.n, self.mine, self.size = (n_dp, me, n_ex) if axis == "dp" else (n_ex, ex, n_dp)
            self.src, self.dst = src, dst.at[q, c]
            self.send, self.recv = send.at[q, c], recv.at[q, c]

        def start(self):
            own = rows(self.mine, self.size)
            pltpu.make_async_copy(self.src.at[own], self.dst.at[own], self.recv).start()

            def go(s, c):
                k = lax.rem(self.mine + s, self.n)
                pltpu.make_async_remote_copy(
                    src_ref=self.src.at[rows(k, self.size)],
                    dst_ref=self.dst.at[own],
                    send_sem=self.send,
                    recv_sem=self.recv,
                    device_id={self.axis: k},
                ).start()
                return c

            lax.fori_loop(1, self.n, go, 0)

        def arrive(self):
            pltpu.make_async_copy(self.src, self.dst, self.recv).wait()

        def drain(self):
            sent = self.src.at[pl.ds(0, (self.n - 1) * self.size)]
            pltpu.make_async_copy(sent, sent, self.send).wait()

    axes = ("dp", "expert")

    def pair_of(q, first, second, r_first, r_second, sems):
        return (
            [Exchange(axes[c], q, c, first(c), r_first, *sems[:2]) for c in range(2)],
            [Exchange(axes[1 - c], q, c, second(c), r_second, *sems[2:]) for c in range(2)],
        )

    def in_pair(q):
        return pair_of(
            q,
            lambda c: b1.at[q] if c else a1.at[q, 0],
            lambda c: a2.at[q, c],
            r1, r2, (s1_sem, r1_sem, s2_sem, r2_sem),
        )

    ins = [in_pair(q) for q in range(2)]

    def by_expert(v):
        return dot(perm[...], v).astype(BF16)

    def by_dp(v):
        return dot(perm[...], v, 0, 0).astype(BF16)

    def fetch(q, src):
        gather(q, src)
        b1[q] = by_expert(a1[q, 1])

    r_id = lax.broadcasted_iota(jnp.int32, (n_rows, n_rows), 0)
    c_id = lax.broadcasted_iota(jnp.int32, (n_rows, n_rows), 1)
    bits = n_dp.bit_length() - 1
    source = (r_id & (n_dp - 1)) * n_ex + lax.shift_right_logical(r_id, bits)
    perm[...] = jnp.where(c_id == source, 1.0, 0.0).astype(BF16)
    fetch(0, tok_v)
    pl.semaphore_wait(barrier, n_dp + n_ex - 2)
    for x in ins[0][0]:
        x.start()
    loads[3].wait()
    fetch(1, dyo_v)
    for x in ins[1][0]:
        x.start()
    for q in range(2):
        first, second = ins[q]
        first[0].arrive()
        a2[q, 0] = by_expert(r1[q, 0])
        second[0].start()
        first[1].arrive()
        a2[q, 1] = by_dp(r1[q, 1])
        second[1].start()

    def settle(q):
        second = ins[q][1]
        second[0].arrive()
        xd[q, :, :lanes] = r2[q, 0]
        second[1].arrive()
        xd[q, :, lanes:] = by_expert(r2[q, 1])

    for load in loads[4:]:
        load.wait()

    def partial(m, value):
        value = value.astype(BF16)
        for c in range(2):
            part[m, c] = value[:, c * hh:(c + 1) * hh].reshape(NX, ny, cap, hh)

    def arm_len(m, c, s):
        return ny // 2 - (m + c + s) % 2

    def sign(s):
        return 1 - 2 * s

    def xa_copy(m, off):
        block = y_of(off)
        return pltpu.make_async_remote_copy(
            src_ref=part.at[m, 0, 1 - xl, block],
            dst_ref=xa.at[m, block],
            send_sem=xas_sem.at[0],
            recv_sem=xar_sem.at[m, off % ny],
            device_id={"dp": pair},
        )

    far_first = sorted(range(-(ny // 2) + 1, ny // 2 + 1), key=lambda o: -abs(o))

    def xa_send(m):
        for off in far_first:
            xa_copy(m, off).start()

    def arm_copy(m, c, s, h):
        arm, acc = ((arm_a, acc_a), (arm_b, acc_b))[c]
        if c == 1 and h == 0:
            src = part.at[m, 1, :, y_of(sign(s) * arm_len(m, c, s))]
        else:
            src = acc.at[m, s, h]
        return pltpu.make_async_remote_copy(
            src_ref=src,
            dst_ref=arm.at[m, s, h],
            send_sem=as_sem.at[c],
            recv_sem=ar_sem.at[m, c, s, h],
            device_id=y_dev(sign(s)),
        )

    def hop(m, c, h):
        for s in range(2):
            n = arm_len(m, c, s)
            if h >= n:
                continue
            off = sign(s) * (n - h)
            owner = y_of(off)
            if c == 0:
                xa_copy(m, off).wait_recv()
                v = part[m, 0, xl, owner].astype(F32) + xa[m, owner].astype(F32)
                if h > 0:
                    arm_copy(m, c, s, h - 1).wait_recv()
                    v = v + arm_a[m, s, h - 1].astype(F32)
                acc_a[m, s, h] = v.astype(BF16)
            elif h > 0:
                arm_copy(m, c, s, h - 1).wait_recv()
                v = part[m, 1, :, owner].astype(F32) + arm_b[m, s, h - 1].astype(F32)
                acc_b[m, s, h] = v.astype(BF16)
            arm_copy(m, c, s, h).start()

    def x_copy(m):
        return pltpu.make_async_remote_copy(
            src_ref=xsend.at[m],
            dst_ref=xrecv.at[m],
            send_sem=xs_sem.at[0],
            recv_sem=xr_sem.at[m],
            device_id={"dp": pair},
        )

    def b_total(m, side):
        v = part[m, 1, side, y].astype(F32)
        for s in range(2):
            v = v + arm_b[m, s, arm_len(m, 1, s) - 1, side].astype(F32)
        return v

    def b_end(m):
        for s in range(2):
            arm_copy(m, 1, s, arm_len(m, 1, s) - 1).wait_recv()
        xsend[m] = b_total(m, 1 - xl).astype(BF16)
        x_copy(m).start()

    def finish(m):
        xa_copy(m, 0).wait_recv()
        v = part[m, 0, xl, y].astype(F32) + xa[m, y].astype(F32)
        for s in range(2):
            n = arm_len(m, 0, s)
            arm_copy(m, 0, s, n - 1).wait_recv()
            v = v + arm_a[m, s, n - 1].astype(F32)
        x_copy(m).wait_recv()
        return jnp.concatenate([v, b_total(m, xl) + xrecv[m].astype(F32)], axis=1)

    last = ny // 2

    settle(0)
    partial(0, dot(xd[0, :, :piece], wg_v[...]))
    xa_send(0)
    hop(0, 1, 0)
    partial(1, dot(xd[0, :, :piece], wu_v[...]))
    xa_send(1)
    hop(1, 1, 0)
    hop(0, 0, 0)
    hop(0, 1, 1)
    settle(1)
    partial(2, dot(xd[1, :, :piece], wd_v[...]))
    xa_send(2)
    hop(2, 1, 0)
    for h in range(1, last + 2):
        for m, c, k in (
            (1, 1, h), (1, 0, h - 1), (0, 0, h), (0, 1, h + 1), (2, 1, h), (2, 0, h - 1)
        ):
            if k < last:
                hop(m, c, k)
            elif k == last and c == 1:
                b_end(m)
    gate_pre = finish(0)
    up_pre = finish(1)
    gate_rows = xd[0, rows(me, cap), :].astype(F32)
    wl = lax.broadcasted_iota(jnp.int32, (cap, width), 1)
    gate_w = jnp.sum(jnp.where(wl == piece, gate_rows, 0.0), axis=1, keepdims=True)
    sig = 1.0 / (1.0 + jnp.exp(-gate_pre))
    act = gate_pre * sig
    hidden = act * up_pre
    slope = up_pre * sig * (1.0 + gate_pre * (1.0 - sig))
    base = finish(2)
    grad_hidden = gate_w * base

    def keep(m, value):
        value = value.astype(BF16)
        for c in range(2):
            q_all[m, c, xl, y] = value[:, c * hh:(c + 1) * hh]

    def q_remote(block, send, recv, device):
        return pltpu.make_async_remote_copy(
            src_ref=block, dst_ref=block, send_sem=send, recv_sem=recv, device_id=device
        )

    def q_xb(m):
        return q_remote(q_all.at[m, 1, xl, y], qxs_sem.at[1], qxr_sem.at[m, 1], {"dp": pair})

    def q_xa(m, off):
        block = q_all.at[m, 0, xl, y_of(off)]
        return q_remote(block, qxs_sem.at[0], qxr_sem.at[m, 0], {"dp": pair})

    def q_arm(m, c, s, h):
        owner = y_of(-sign(s) * h)
        block = q_all.at[m, 0, xl, owner] if c == 0 else q_all.at[m, 1, :, owner]
        return q_remote(block, qs_sem.at[c], qr_sem.at[m, c, s, h], y_dev(sign(s)))

    def q_hop(m, c, h):
        if h == 0:
            if c == 0:
                q_xa(m, 0).start()
            else:
                q_xb(m).wait_recv()
        for s in range(2):
            n = arm_len(m, c, s)
            if h > n:
                continue
            if h > 0:
                q_arm(m, c, s, h - 1).wait_recv()
            if h < n:
                q_arm(m, c, s, h).start()
            if c == 0 and h > 0:
                q_xa(m, -sign(s) * h).start()

    def q_end(m):
        side = q_all.at[m, 0, 1 - xl]
        pltpu.make_async_copy(side, side, qxr_sem.at[m, 0]).wait()

    keep(1, grad_hidden * slope)
    q_xb(1).start()
    q_hop(1, 0, 0)
    keep(2, grad_hidden * act)
    q_xb(2).start()
    q_hop(2, 0, 0)
    q_hop(1, 1, 0)
    q_hop(2, 1, 0)
    keep(0, gate_w * hidden)
    own_gg[...] = jnp.broadcast_to(jnp.sum(hidden * base, axis=1, keepdims=True), own_gg.shape)
    for h in range(1, last + 1):
        for m in (1, 2):
            q_hop(m, 0, h)
            q_hop(m, 1, h)
    q_xb(0).start()
    q_end(1)
    q_end(2)

    def back(m):
        return jnp.concatenate(
            [q_all[m, c].reshape(n_rows, hh) for c in range(2)], axis=1
        )

    grad_rows[:, width - 128:] = jnp.zeros((n_rows, 128), BF16)
    grad_rows[:, :piece] = (
        dot(back(1), wg_v[...], 1, 1) + dot(back(2), wu_v[...], 1, 1)
    ).astype(BF16)
    tail = grad_rows[rows(me, cap), width - 128:].astype(F32)
    tl = lax.broadcasted_iota(jnp.int32, tail.shape, 1) + (width - 128)
    rest = own_gg[...]
    for n in range(3):
        top = rest.astype(BF16).astype(F32)
        tail = jnp.where(tl == piece + n, top, tail)
        rest = rest - top
    grad_rows[rows(me, cap), width - 128:] = tail.astype(BF16)

    home = [
        Exchange("expert", 0, 0, a3.at[0], r3, s3_sem, r3_sem),
        Exchange("dp", 0, 1, a3.at[1], r3, s3_sem, r3_sem),
    ]
    home2 = [
        Exchange("dp", 0, 0, a4.at[0], r4, s4_sem, r4_sem),
        Exchange("expert", 0, 1, a4.at[1], r4, s4_sem, r4_sem),
    ]
    a3[0] = grad_rows[:, :lanes]
    home[0].start()
    a3[1] = by_dp(grad_rows[:, lanes:])
    home[1].start()

    outs = [
        pltpu.make_async_copy(gw_v.at[m], dst, out_sem.at[m])
        for m, dst in ((1, gwg_out), (2, gwu_out), (0, gwd_out))
    ]
    q_hop(0, 0, 0)
    q_hop(0, 1, 0)
    gw_v[1] = dot(xd[0, :, :piece], back(1), 0, 0).astype(BF16)
    outs[0].start()
    q_hop(0, 0, 1)
    q_hop(0, 1, 1)
    gw_v[2] = dot(xd[0, :, :piece], back(2), 0, 0).astype(BF16)
    outs[1].start()
    for h in range(2, last):
        q_hop(0, 0, h)
        q_hop(0, 1, h)
    home[0].arrive()
    a4[0] = by_dp(r3[0, 0])
    home2[0].start()
    home[1].arrive()
    a4[1] = by_expert(r3[0, 1])
    home2[1].start()
    q_hop(0, 0, last)
    q_hop(0, 1, last)
    q_end(0)
    gw_v[0] = dot(xd[1, :, :piece], back(0), 0, 0).astype(BF16)
    outs[2].start()
    for x in home2:
        x.arrive()

    for x in (*ins[0][0], *ins[0][1], *ins[1][0], *ins[1][1], *home, *home2):
        x.drain()

    def sent(ref, sem):
        pltpu.make_async_copy(ref, ref, sem).wait()

    sent(part.at[:, 0, 0], xas_sem.at[0])
    sent(part.at[:, 0, 0, pl.ds(0, ny - 1)], as_sem.at[0])
    sent(part.at[:, 1, :, pl.ds(0, ny - 1)], as_sem.at[1])
    sent(xsend, xs_sem.at[0])
    sent(part.at[:, 0, 0], qxs_sem.at[0])
    sent(xsend, qxs_sem.at[1])
    sent(part.at[:, 0, 0, pl.ds(0, ny - 1)], qs_sem.at[0])
    sent(part.at[:, 1, :, pl.ds(0, ny - 1)], qs_sem.at[1])
    for out in outs:
        out.wait()


def last_kernel(
    cfg, r4, route, gwg, gwu, gwd, gt_out, gg_out, gwg_out, gwu_out, gwd_out,
    r4_v, late, route_v, gw_v, wide, gt_v, gg_v, in_sem, out_sem,
):
    n_dp, n_ex, piece, width, hid = cfg
    d_model = n_dp * piece
    win = width + 128
    ins = [
        pltpu.make_async_copy(src, dst, in_sem.at[n])
        for n, (src, dst) in enumerate(
            [(r4, r4_v), (route, route_v)]
            + [(src, gw_v.at[m]) for m, src in enumerate((gwg, gwu, gwd))]
        )
    ]
    outs = [
        pltpu.make_async_copy(src, dst, out_sem.at[n])
        for n, (src, dst) in enumerate(
            [(gw_v.at[m], dst) for m, dst in enumerate((gwg_out, gwu_out, gwd_out))]
            + [(gg_v, gg_out), (gt_v, gt_out)]
        )
    ]
    for copy in ins:
        copy.start()
    wide[...] = jnp.zeros(wide.shape, F32)
    ins[0].wait()
    ins[1].wait()
    late[...] = r4_v[0, 1].astype(F32)
    lane = lax.broadcasted_iota(jnp.int32, (n_ex, width), 1)
    sums = jnp.zeros((n_ex, width), F32)
    for d in range(n_dp):
        start = (piece * d) // 128 * 128
        shift = piece * d - start
        v = jnp.concatenate(
            [
                r4_v[0, 0, d * n_ex:(d + 1) * n_ex, :].astype(F32),
                late[pl.ds(d, n_ex, stride=n_dp), :],
            ],
            axis=1,
        )
        sums = sums + jnp.where((lane >= piece) & (lane < piece + 3), v, 0.0)
        v = jnp.concatenate([jnp.where(lane < piece, v, 0.0), jnp.zeros((n_ex, 128), F32)], axis=1)
        if shift:
            v = pltpu.roll(v, shift, 1)
        wide[:, start:start + win] += v
    for n in range(3):
        ins[2 + n].wait()
        outs[n].start()
    e_row = lax.broadcasted_iota(jnp.int32, (n_ex, n_ex), 0)
    e_col = lax.broadcasted_iota(jnp.int32, (n_ex, n_ex), 1)
    column = jnp.broadcast_to(jnp.sum(sums, axis=1, keepdims=True), (n_ex, n_ex))
    gg_v[...] = jnp.sum(jnp.where(e_row == e_col, column, 0.0), axis=0, keepdims=True)
    outs[3].start()
    pick = one_hot_rows(route_v[...], gt_v.shape[0])
    gt_v[...] = dot(pick, wide[:, :d_model].astype(BF16)).astype(BF16)
    outs[4].start()
    for copy in outs:
        copy.wait()


def local(tokens, grad_out, route, gates, w_gate, w_up, w_down):
    n_dp = lax.axis_size("dp")
    n_ex = lax.axis_size("expert")
    piece, hid = w_gate.shape[1:]
    tok_dev, d_model = tokens.shape
    width = (piece + 3 + 127) // 128 * 128
    n_rows = n_dp * n_ex
    ny = n_dp // NX
    hops = ny // 2
    cap = n_ex
    hh = hid // 2
    dma = pltpu.SemaphoreType.DMA
    any_spec = pl.BlockSpec(memory_space=pl.ANY)
    cfg = (n_dp, n_ex, piece, width, hid)
    weights = jax.ShapeDtypeStruct((piece, hid), BF16)
    route_row = route.reshape(1, n_ex)
    wide = pltpu.VMEM((n_ex, d_model + width + 128), F32)
    lanes = width // 2
    whole = pltpu.VMEM((2, n_rows, width), BF16)
    block = pltpu.VMEM((2, 2, n_rows, lanes), BF16)
    halves = pltpu.VMEM((2, n_rows, lanes), BF16)
    r4, gwg, gwu, gwd = pl.pallas_call(
        functools.partial(kernel, cfg),
        out_shape=(jax.ShapeDtypeStruct((1, 2, n_rows, lanes), BF16), weights, weights, weights),
        in_specs=[any_spec] * 7,
        out_specs=(any_spec,) * 4,
        scratch_shapes=[
            pltpu.VMEM((tok_dev, d_model), BF16),
            pltpu.VMEM((tok_dev, d_model), BF16),
            pltpu.VMEM((piece, hid), BF16),
            pltpu.VMEM((piece, hid), BF16),
            pltpu.VMEM((piece, hid), BF16),
            pltpu.VMEM((1, n_ex), jnp.int32),
            pltpu.VMEM((1, n_ex), BF16),
            wide,
            pltpu.VMEM((n_rows, n_rows), BF16),
            block, halves, block, block, block, whole,
            pltpu.VMEM((3, 2, NX, ny, cap, hh), BF16),
            pltpu.VMEM((3, ny, cap, hh), BF16),
            pltpu.VMEM((3, 2, hops, cap, hh), BF16),
            pltpu.VMEM((3, 2, hops, cap, hh), BF16),
            pltpu.VMEM((3, 2, hops, NX, cap, hh), BF16),
            pltpu.VMEM((3, 2, hops, NX, cap, hh), BF16),
            pltpu.VMEM((3, cap, hh), BF16),
            pltpu.VMEM((3, cap, hh), BF16),
            pltpu.VMEM((3, 2, NX, ny, cap, hh), BF16),
            pltpu.VMEM((cap, 128), F32),
            pltpu.VMEM((n_rows, width), BF16),
            halves,
            pltpu.VMEM((1, 2, n_rows, lanes), BF16),
            halves,
            pltpu.VMEM((3, piece, hid), BF16),
            dma((7,)),
            dma((2, 2)), dma((2, 2)),
            dma((2, 2)), dma((2, 2)),
            dma((1,)), dma((3, ny)),
            dma((2,)), dma((3, 2, 2, hops)),
            dma((1,)), dma((3,)),
            dma((2,)), dma((3, 2, 2, hops)),
            dma((2,)), dma((3, 2)),
            dma((1, 2)), dma((1, 2)),
            dma((1, 2)), dma((1, 2)),
            dma((3,)),
        ],
        compiler_params=pltpu.CompilerParams(
            collective_id=0, has_side_effects=True, vmem_limit_bytes=56 * 1024 * 1024
        ),
        name="moe",
    )(
        tokens,
        grad_out,
        route_row,
        gates.reshape(1, n_ex),
        w_gate[0],
        w_up[0],
        jnp.swapaxes(w_down[0], 0, 1),
    )
    gt, gg, gwg, gwu, gwd = pl.pallas_call(
        functools.partial(last_kernel, cfg),
        out_shape=(
            jax.ShapeDtypeStruct((tok_dev, d_model), BF16),
            jax.ShapeDtypeStruct((1, n_ex), F32),
            weights, weights, weights,
        ),
        in_specs=[any_spec] * 5,
        out_specs=(any_spec,) * 5,
        scratch_shapes=[
            pltpu.VMEM((1, 2, n_rows, lanes), BF16),
            pltpu.VMEM((n_rows, lanes), F32),
            pltpu.VMEM((1, n_ex), jnp.int32),
            pltpu.VMEM((3, piece, hid), BF16),
            wide,
            pltpu.VMEM((tok_dev, d_model), BF16),
            pltpu.VMEM((1, n_ex), F32),
            dma((5,)),
            dma((5,)),
        ],
        compiler_params=pltpu.CompilerParams(vmem_limit_bytes=56 * 1024 * 1024),
        name="scatter",
    )(r4, route_row, gwg, gwu, gwd)
    return (
        gt, gwg[None], gwu[None], jnp.swapaxes(gwd, 0, 1)[None], gg.reshape(gates.shape),
    )


def solution(mesh):
    return jax.shard_map(
        local,
        mesh=mesh,
        in_specs=(
            P(("dp", "expert"), None),
            P(("dp", "expert"), None),
            P("dp", "expert", None, None),
            P("dp", "expert", None, None),
            P("expert", "dp", None),
            P("expert", "dp", None),
            P("expert", None, "dp"),
        ),
        out_specs=(
            P(("dp", "expert"), None),
            P("expert", "dp", None),
            P("expert", "dp", None),
            P("expert", None, "dp"),
            P("dp", "expert", None, None),
        ),
        check_vma=False,
    )
```

```python
import functools

import jax
import jax.numpy as jnp
from jax import lax
from jax.experimental import pallas as pl
from jax.experimental.pallas import tpu as pltpu
from jax.sharding import PartitionSpec as P

NX = 2
F32 = jnp.float32
BF16 = jnp.bfloat16


def dot(a, b, ca=1, cb=0):
    return lax.dot_general(a, b, (((ca,), (cb,)), ((), ())), preferred_element_type=F32)


def one_hot_rows(route, tok_dev):
    n_ex = route.shape[1]
    t_id = lax.broadcasted_iota(jnp.int32, (tok_dev, n_ex), 0)
    return jnp.where(t_id == jnp.broadcast_to(route, (tok_dev, n_ex)), 1.0, 0.0).astype(BF16)


def kernel(
    cfg,
    tokens, grad_out, route, gates, wg, wu, wd,
    r4, gwg_out, gwu_out, gwd_out,
    tok_v, dyo_v, wg_v, wu_v, wd_v, route_v, gates_v, wide, perm, a1, b1, r1, a2, r2, xd,
    part, xa, arm_a, acc_a, arm_b, acc_b, xsend, xrecv, q_all, own_gg, grad_rows, a3, r3, a4, gw_v,
    load_sem, s1_sem, r1_sem, s2_sem, r2_sem, xas_sem, xar_sem, as_sem, ar_sem, xs_sem, xr_sem,
    qs_sem, qr_sem, qxs_sem, qxr_sem, s3_sem, r3_sem, s4_sem, r4_sem, out_sem,
):
    n_dp, n_ex, piece, width, hid = cfg
    ny = n_dp // NX
    n_rows = n_dp * n_ex
    d_model = n_dp * piece
    cap = n_ex
    hh = hid // 2
    win = width + 128
    lanes = width // 2

    me = lax.axis_index("dp")
    ex = lax.axis_index("expert")
    xl = me // ny
    y = lax.rem(me, ny)
    pair = (1 - xl) * ny + y

    def y_of(off):
        return lax.rem(y + off + 2 * ny, ny)

    def y_dev(off):
        return {"dp": xl * ny + y_of(off)}

    def rows(k, n):
        return pl.ds(pl.multiple_of(k * n, n), n)

    barrier = pltpu.get_barrier_semaphore()

    def greet_dp(s, c):
        pl.semaphore_signal(barrier, inc=1, device_id={"dp": lax.rem(me + s, n_dp)})
        return c

    def greet_ex(s, c):
        pl.semaphore_signal(barrier, inc=1, device_id={"expert": lax.rem(ex + s, n_ex)})
        return c

    lax.fori_loop(1, n_ex, greet_ex, 0)
    lax.fori_loop(1, n_dp, greet_dp, 0)

    loads = [
        pltpu.make_async_copy(src, dst, load_sem.at[n])
        for n, (src, dst) in enumerate(
            [
                (route, route_v), (gates, gates_v), (tokens, tok_v), (grad_out, dyo_v),
                (wg, wg_v), (wu, wu_v), (wd, wd_v),
            ]
        )
    ]
    for load in loads:
        load.start()

    lane = lax.broadcasted_iota(jnp.int32, (n_ex, width), 1)
    wide[:, d_model:] = jnp.zeros((n_ex, wide.shape[1] - d_model), F32)
    for load in loads[:3]:
        load.wait()
    pick = one_hot_rows(route_v[...], tok_v.shape[0])
    e_row = lax.broadcasted_iota(jnp.int32, (n_ex, n_ex), 0)
    e_col = lax.broadcasted_iota(jnp.int32, (n_ex, n_ex), 1)
    gate_row = jnp.broadcast_to(gates_v[...].astype(F32), (n_ex, n_ex))
    gate_own = jnp.sum(jnp.where(e_row == e_col, gate_row, 0.0), axis=1, keepdims=True)

    def gather(q, src):
        wide[:, :d_model] = dot(pick, src[...], 0, 0)
        for d in range(n_dp):
            start = (piece * d) // 128 * 128
            shift = piece * d - start
            v = wide[:, start:start + win]
            if shift:
                v = pltpu.roll(v, win - shift, 1)
            v = v[:, :width]
            pad = jnp.where(lane == piece, gate_own, 0.0) if q == 0 else 0.0
            v = jnp.where(lane < piece, v, pad).astype(BF16)
            for c in range(2):
                a1[q, c, d * n_ex:(d + 1) * n_ex, :] = v[:, c * lanes:(c + 1) * lanes]

    class Exchange:
        def __init__(self, axis, q, c, src, dst, send, recv):
            self.axis = axis
            self.n, self.mine, self.size = (n_dp, me, n_ex) if axis == "dp" else (n_ex, ex, n_dp)
            self.src, self.dst = src, dst.at[q, c]
            self.send, self.recv = send.at[q, c], recv.at[q, c]

        def start(self):
            own = rows(self.mine, self.size)
            pltpu.make_async_copy(self.src.at[own], self.dst.at[own], self.recv).start()

            def go(s, c):
                k = lax.rem(self.mine + s, self.n)
                pltpu.make_async_remote_copy(
                    src_ref=self.src.at[rows(k, self.size)],
                    dst_ref=self.dst.at[own],
                    send_sem=self.send,
                    recv_sem=self.recv,
                    device_id={self.axis: k},
                ).start()
                return c

            lax.fori_loop(1, self.n, go, 0)

        def arrive(self):
            pltpu.make_async_copy(self.src, self.dst, self.recv).wait()

        def drain(self):
            sent = self.src.at[pl.ds(0, (self.n - 1) * self.size)]
            pltpu.make_async_copy(sent, sent, self.send).wait()

    axes = ("dp", "expert")

    def pair_of(q, first, second, r_first, r_second, sems):
        return (
            [Exchange(axes[c], q, c, first(c), r_first, *sems[:2]) for c in range(2)],
            [Exchange(axes[1 - c], q, c, second(c), r_second, *sems[2:]) for c in range(2)],
        )

    def in_pair(q):
        return pair_of(
            q,
            lambda c: b1.at[q] if c else a1.at[q, 0],
            lambda c: a2.at[q, c],
            r1, r2, (s1_sem, r1_sem, s2_sem, r2_sem),
        )

    ins = [in_pair(q) for q in range(2)]

    def by_expert(v):
        return dot(perm[...], v).astype(BF16)

    def by_dp(v):
        return dot(perm[...], v, 0, 0).astype(BF16)

    def fetch(q, src):
        gather(q, src)
        b1[q] = by_expert(a1[q, 1])

    r_id = lax.broadcasted_iota(jnp.int32, (n_rows, n_rows), 0)
    c_id = lax.broadcasted_iota(jnp.int32, (n_rows, n_rows), 1)
    bits = n_dp.bit_length() - 1
    source = (r_id & (n_dp - 1)) * n_ex + lax.shift_right_logical(r_id, bits)
    perm[...] = jnp.where(c_id == source, 1.0, 0.0).astype(BF16)
    fetch(0, tok_v)
    pl.semaphore_wait(barrier, n_dp + n_ex - 2)
    for x in ins[0][0]:
        x.start()
    loads[3].wait()
    fetch(1, dyo_v)
    for x in ins[1][0]:
        x.start()
    for q in range(2):
        first, second = ins[q]
        first[0].arrive()
        a2[q, 0] = by_expert(r1[q, 0])
        second[0].start()
        first[1].arrive()
        a2[q, 1] = by_dp(r1[q, 1])
        second[1].start()

    def settle(q):
        second = ins[q][1]
        second[0].arrive()
        xd[q, :, :lanes] = r2[q, 0]
        second[1].arrive()
        xd[q, :, lanes:] = by_expert(r2[q, 1])

    for load in loads[4:]:
        load.wait()

    def partial(m, value):
        value = value.astype(BF16)
        for c in range(2):
            part[m, c] = value[:, c * hh:(c + 1) * hh].reshape(NX, ny, cap, hh)

    def arm_len(m, c, s):
        return ny // 2 - (m + c + s) % 2

    def sign(s):
        return 1 - 2 * s

    def xa_copy(m, off):
        block = y_of(off)
        return pltpu.make_async_remote_copy(
            src_ref=part.at[m, 0, 1 - xl, block],
            dst_ref=xa.at[m, block],
            send_sem=xas_sem.at[0],
            recv_sem=xar_sem.at[m, off % ny],
            device_id={"dp": pair},
        )

    def xa_send(m, level):
        long = sign(m % 2)
        n = ny // 2 - level
        for off in {1: (long,), 0: (0,)}.get(n, (n * long, (1 - n) * long)):
            xa_copy(m, off).start()

    def arm_copy(m, c, s, h):
        arm, acc = ((arm_a, acc_a), (arm_b, acc_b))[c]
        if c == 1 and h == 0:
            src = part.at[m, 1, :, y_of(sign(s) * arm_len(m, c, s))]
        else:
            src = acc.at[m, s, h]
        return pltpu.make_async_remote_copy(
            src_ref=src,
            dst_ref=arm.at[m, s, h],
            send_sem=as_sem.at[c],
            recv_sem=ar_sem.at[m, c, s, h],
            device_id=y_dev(sign(s)),
        )

    def hop(m, c, h):
        for s in range(2):
            n = arm_len(m, c, s)
            if h >= n:
                continue
            off = sign(s) * (n - h)
            owner = y_of(off)
            if c == 0:
                xa_copy(m, off).wait_recv()
                v = part[m, 0, xl, owner].astype(F32) + xa[m, owner].astype(F32)
                if h > 0:
                    arm_copy(m, c, s, h - 1).wait_recv()
                    v = v + arm_a[m, s, h - 1].astype(F32)
                acc_a[m, s, h] = v.astype(BF16)
            elif h > 0:
                arm_copy(m, c, s, h - 1).wait_recv()
                v = part[m, 1, :, owner].astype(F32) + arm_b[m, s, h - 1].astype(F32)
                acc_b[m, s, h] = v.astype(BF16)
            arm_copy(m, c, s, h).start()

    def x_copy(m):
        return pltpu.make_async_remote_copy(
            src_ref=xsend.at[m],
            dst_ref=xrecv.at[m],
            send_sem=xs_sem.at[0],
            recv_sem=xr_sem.at[m],
            device_id={"dp": pair},
        )

    def b_total(m, side):
        v = part[m, 1, side, y].astype(F32)
        for s in range(2):
            v = v + arm_b[m, s, arm_len(m, 1, s) - 1, side].astype(F32)
        return v

    def b_end(m):
        for s in range(2):
            arm_copy(m, 1, s, arm_len(m, 1, s) - 1).wait_recv()
        xsend[m] = b_total(m, 1 - xl).astype(BF16)
        x_copy(m).start()

    def end_a(m):
        xa_copy(m, 0).wait_recv()
        v = part[m, 0, xl, y].astype(F32) + xa[m, y].astype(F32)
        for s in range(2):
            n = arm_len(m, 0, s)
            arm_copy(m, 0, s, n - 1).wait_recv()
            v = v + arm_a[m, s, n - 1].astype(F32)
        return v

    def end_b(m):
        x_copy(m).wait_recv()
        return b_total(m, xl) + xrecv[m].astype(F32)

    last = ny // 2

    settle(0)
    partial(0, dot(xd[0, :, :piece], wg_v[...]))
    hop(0, 1, 0)
    xa_send(0, 0)
    partial(1, dot(xd[0, :, :piece], wu_v[...]))
    hop(1, 1, 0)
    xa_send(1, 0)
    xa_send(0, 1)
    xa_send(1, 1)
    settle(1)
    partial(2, dot(xd[1, :, :piece], wd_v[...]))
    hop(2, 1, 0)
    xa_send(2, 0)
    xa_send(2, 1)
    for level in range(2, last + 1):
        for m in range(3):
            xa_send(m, level)
    for h in range(1, last + 1):
        for m in range(3):
            if h < last:
                hop(m, 1, h)
            else:
                b_end(m)
        for m in range(3):
            hop(m, 0, h - 1)

    gate_rows = xd[0, rows(me, cap), :].astype(F32)
    wl = lax.broadcasted_iota(jnp.int32, (cap, width), 1)
    gate_w = jnp.sum(jnp.where(wl == piece, gate_rows, 0.0), axis=1, keepdims=True)

    def activate(c, end):
        gate_pre = end(0)
        up_pre = end(1)
        sig = 1.0 / (1.0 + jnp.exp(-gate_pre))
        act = gate_pre * sig
        hidden = act * up_pre
        slope = up_pre * sig * (1.0 + gate_pre * (1.0 - sig))
        base = end(2)
        grad_hidden = gate_w * base
        q_all[1, c, xl, y] = (grad_hidden * slope).astype(BF16)
        q_all[2, c, xl, y] = (grad_hidden * act).astype(BF16)
        q_all[0, c, xl, y] = (gate_w * hidden).astype(BF16)
        return jnp.sum(hidden * base, axis=1, keepdims=True)

    def q_remote(block, send, recv, device):
        return pltpu.make_async_remote_copy(
            src_ref=block, dst_ref=block, send_sem=send, recv_sem=recv, device_id=device
        )

    def q_xb(m):
        return q_remote(q_all.at[m, 1, xl, y], qxs_sem.at[1], qxr_sem.at[m, 1], {"dp": pair})

    def q_xa(m, off):
        block = q_all.at[m, 0, xl, y_of(off)]
        return q_remote(block, qxs_sem.at[0], qxr_sem.at[m, 0], {"dp": pair})

    def q_arm(m, c, s, h):
        owner = y_of(-sign(s) * h)
        block = q_all.at[m, 0, xl, owner] if c == 0 else q_all.at[m, 1, :, owner]
        return q_remote(block, qs_sem.at[c], qr_sem.at[m, c, s, h], y_dev(sign(s)))

    def q_hop(m, c, h):
        if h == 0:
            if c == 0:
                q_xa(m, 0).start()
            else:
                q_xb(m).wait_recv()
        for s in range(2):
            n = arm_len(m, c, s)
            if h > n:
                continue
            if h > 0:
                q_arm(m, c, s, h - 1).wait_recv()
            if h < n:
                q_arm(m, c, s, h).start()
            if c == 0 and h > 0:
                q_xa(m, -sign(s) * h).start()

    def q_end(m):
        side = q_all.at[m, 0, 1 - xl]
        pltpu.make_async_copy(side, side, qxr_sem.at[m, 0]).wait()

    gg = activate(1, end_b)
    for m in (1, 2, 0):
        q_xb(m).start()
    gg = gg + activate(0, end_a)
    own_gg[...] = jnp.broadcast_to(gg, own_gg.shape)
    for m in (1, 2):
        q_hop(m, 1, 0)
        q_hop(m, 0, 0)
    for h in range(1, last + 1):
        for m, k in ((1, h), (2, h), (0, h - 1)):
            q_hop(m, 1, k)
            q_hop(m, 0, k)
    q_end(1)
    q_end(2)

    def back(m):
        return jnp.concatenate(
            [q_all[m, c].reshape(n_rows, hh) for c in range(2)], axis=1
        )

    grad_rows[:, width - 128:] = jnp.zeros((n_rows, 128), BF16)
    grad_rows[:, :piece] = (
        dot(back(1), wg_v[...], 1, 1) + dot(back(2), wu_v[...], 1, 1)
    ).astype(BF16)
    tail = grad_rows[rows(me, cap), width - 128:].astype(F32)
    tl = lax.broadcasted_iota(jnp.int32, tail.shape, 1) + (width - 128)
    rest = own_gg[...]
    for n in range(3):
        top = rest.astype(BF16).astype(F32)
        tail = jnp.where(tl == piece + n, top, tail)
        rest = rest - top
    grad_rows[rows(me, cap), width - 128:] = tail.astype(BF16)

    home = [
        Exchange("expert", 0, 0, a3.at[0], r3, s3_sem, r3_sem),
        Exchange("dp", 0, 1, a3.at[1], r3, s3_sem, r3_sem),
    ]
    home2 = [
        Exchange("dp", 0, 0, a4.at[0], r4, s4_sem, r4_sem),
        Exchange("expert", 0, 1, a4.at[1], r4, s4_sem, r4_sem),
    ]
    a3[0] = grad_rows[:, :lanes]
    home[0].start()
    a3[1] = by_dp(grad_rows[:, lanes:])
    home[1].start()

    outs = [
        pltpu.make_async_copy(gw_v.at[m], dst, out_sem.at[m])
        for m, dst in ((1, gwg_out), (2, gwu_out), (0, gwd_out))
    ]
    q_hop(0, 1, last)
    q_hop(0, 0, last)
    gw_v[1] = dot(xd[0, :, :piece], back(1), 0, 0).astype(BF16)
    outs[0].start()
    gw_v[2] = dot(xd[0, :, :piece], back(2), 0, 0).astype(BF16)
    outs[1].start()
    home[0].arrive()
    a4[0] = by_dp(r3[0, 0])
    home2[0].start()
    home[1].arrive()
    a4[1] = by_expert(r3[0, 1])
    home2[1].start()
    q_end(0)
    gw_v[0] = dot(xd[1, :, :piece], back(0), 0, 0).astype(BF16)
    outs[2].start()
    for x in home2:
        x.arrive()

    for x in (*ins[0][0], *ins[0][1], *ins[1][0], *ins[1][1], *home, *home2):
        x.drain()

    def sent(ref, sem):
        pltpu.make_async_copy(ref, ref, sem).wait()

    sent(part.at[:, 0, 0], xas_sem.at[0])
    sent(part.at[:, 0, 0, pl.ds(0, ny - 1)], as_sem.at[0])
    sent(part.at[:, 1, :, pl.ds(0, ny - 1)], as_sem.at[1])
    sent(xsend, xs_sem.at[0])
    sent(part.at[:, 0, 0], qxs_sem.at[0])
    sent(xsend, qxs_sem.at[1])
    sent(part.at[:, 0, 0, pl.ds(0, ny - 1)], qs_sem.at[0])
    sent(part.at[:, 1, :, pl.ds(0, ny - 1)], qs_sem.at[1])
    for out in outs:
        out.wait()


def last_kernel(
    cfg, r4, route, gwg, gwu, gwd, gt_out, gg_out, gwg_out, gwu_out, gwd_out,
    r4_v, late, route_v, gw_v, wide, gt_v, gg_v, in_sem, out_sem,
):
    n_dp, n_ex, piece, width, hid = cfg
    d_model = n_dp * piece
    win = width + 128
    ins = [
        pltpu.make_async_copy(src, dst, in_sem.at[n])
        for n, (src, dst) in enumerate(
            [(r4, r4_v), (route, route_v)]
            + [(src, gw_v.at[m]) for m, src in enumerate((gwg, gwu, gwd))]
        )
    ]
    outs = [
        pltpu.make_async_copy(src, dst, out_sem.at[n])
        for n, (src, dst) in enumerate(
            [(gw_v.at[m], dst) for m, dst in enumerate((gwg_out, gwu_out, gwd_out))]
            + [(gg_v, gg_out), (gt_v, gt_out)]
        )
    ]
    for copy in ins:
        copy.start()
    wide[...] = jnp.zeros(wide.shape, F32)
    ins[0].wait()
    ins[1].wait()
    late[...] = r4_v[0, 1].astype(F32)
    lane = lax.broadcasted_iota(jnp.int32, (n_ex, width), 1)
    sums = jnp.zeros((n_ex, width), F32)
    for d in range(n_dp):
        start = (piece * d) // 128 * 128
        shift = piece * d - start
        v = jnp.concatenate(
            [
                r4_v[0, 0, d * n_ex:(d + 1) * n_ex, :].astype(F32),
                late[pl.ds(d, n_ex, stride=n_dp), :],
            ],
            axis=1,
        )
        sums = sums + jnp.where((lane >= piece) & (lane < piece + 3), v, 0.0)
        v = jnp.concatenate([jnp.where(lane < piece, v, 0.0), jnp.zeros((n_ex, 128), F32)], axis=1)
        if shift:
            v = pltpu.roll(v, shift, 1)
        wide[:, start:start + win] += v
    for n in range(3):
        ins[2 + n].wait()
        outs[n].start()
    e_row = lax.broadcasted_iota(jnp.int32, (n_ex, n_ex), 0)
    e_col = lax.broadcasted_iota(jnp.int32, (n_ex, n_ex), 1)
    column = jnp.broadcast_to(jnp.sum(sums, axis=1, keepdims=True), (n_ex, n_ex))
    gg_v[...] = jnp.sum(jnp.where(e_row == e_col, column, 0.0), axis=0, keepdims=True)
    outs[3].start()
    pick = one_hot_rows(route_v[...], gt_v.shape[0])
    gt_v[...] = dot(pick, wide[:, :d_model].astype(BF16)).astype(BF16)
    outs[4].start()
    for copy in outs:
        copy.wait()


def local(tokens, grad_out, route, gates, w_gate, w_up, w_down):
    n_dp = lax.axis_size("dp")
    n_ex = lax.axis_size("expert")
    piece, hid = w_gate.shape[1:]
    tok_dev, d_model = tokens.shape
    width = (piece + 3 + 127) // 128 * 128
    n_rows = n_dp * n_ex
    ny = n_dp // NX
    hops = ny // 2
    cap = n_ex
    hh = hid // 2
    dma = pltpu.SemaphoreType.DMA
    any_spec = pl.BlockSpec(memory_space=pl.ANY)
    cfg = (n_dp, n_ex, piece, width, hid)
    weights = jax.ShapeDtypeStruct((piece, hid), BF16)
    route_row = route.reshape(1, n_ex)
    wide = pltpu.VMEM((n_ex, d_model + width + 128), F32)
    lanes = width // 2
    whole = pltpu.VMEM((2, n_rows, width), BF16)
    block = pltpu.VMEM((2, 2, n_rows, lanes), BF16)
    halves = pltpu.VMEM((2, n_rows, lanes), BF16)
    r4, gwg, gwu, gwd = pl.pallas_call(
        functools.partial(kernel, cfg),
        out_shape=(jax.ShapeDtypeStruct((1, 2, n_rows, lanes), BF16), weights, weights, weights),
        in_specs=[any_spec] * 7,
        out_specs=(any_spec,) * 4,
        scratch_shapes=[
            pltpu.VMEM((tok_dev, d_model), BF16),
            pltpu.VMEM((tok_dev, d_model), BF16),
            pltpu.VMEM((piece, hid), BF16),
            pltpu.VMEM((piece, hid), BF16),
            pltpu.VMEM((piece, hid), BF16),
            pltpu.VMEM((1, n_ex), jnp.int32),
            pltpu.VMEM((1, n_ex), BF16),
            wide,
            pltpu.VMEM((n_rows, n_rows), BF16),
            block, halves, block, block, block, whole,
            pltpu.VMEM((3, 2, NX, ny, cap, hh), BF16),
            pltpu.VMEM((3, ny, cap, hh), BF16),
            pltpu.VMEM((3, 2, hops, cap, hh), BF16),
            pltpu.VMEM((3, 2, hops, cap, hh), BF16),
            pltpu.VMEM((3, 2, hops, NX, cap, hh), BF16),
            pltpu.VMEM((3, 2, hops, NX, cap, hh), BF16),
            pltpu.VMEM((3, cap, hh), BF16),
            pltpu.VMEM((3, cap, hh), BF16),
            pltpu.VMEM((3, 2, NX, ny, cap, hh), BF16),
            pltpu.VMEM((cap, 128), F32),
            pltpu.VMEM((n_rows, width), BF16),
            halves,
            pltpu.VMEM((1, 2, n_rows, lanes), BF16),
            halves,
            pltpu.VMEM((3, piece, hid), BF16),
            dma((7,)),
            dma((2, 2)), dma((2, 2)),
            dma((2, 2)), dma((2, 2)),
            dma((1,)), dma((3, ny)),
            dma((2,)), dma((3, 2, 2, hops)),
            dma((1,)), dma((3,)),
            dma((2,)), dma((3, 2, 2, hops)),
            dma((2,)), dma((3, 2)),
            dma((1, 2)), dma((1, 2)),
            dma((1, 2)), dma((1, 2)),
            dma((3,)),
        ],
        compiler_params=pltpu.CompilerParams(
            collective_id=0, has_side_effects=True, vmem_limit_bytes=56 * 1024 * 1024
        ),
        name="moe",
    )(
        tokens,
        grad_out,
        route_row,
        gates.reshape(1, n_ex),
        w_gate[0],
        w_up[0],
        jnp.swapaxes(w_down[0], 0, 1),
    )
    gt, gg, gwg, gwu, gwd = pl.pallas_call(
        functools.partial(last_kernel, cfg),
        out_shape=(
            jax.ShapeDtypeStruct((tok_dev, d_model), BF16),
            jax.ShapeDtypeStruct((1, n_ex), F32),
            weights, weights, weights,
        ),
        in_specs=[any_spec] * 5,
        out_specs=(any_spec,) * 5,
        scratch_shapes=[
            pltpu.VMEM((1, 2, n_rows, lanes), BF16),
            pltpu.VMEM((n_rows, lanes), F32),
            pltpu.VMEM((1, n_ex), jnp.int32),
            pltpu.VMEM((3, piece, hid), BF16),
            wide,
            pltpu.VMEM((tok_dev, d_model), BF16),
            pltpu.VMEM((1, n_ex), F32),
            dma((5,)),
            dma((5,)),
        ],
        compiler_params=pltpu.CompilerParams(vmem_limit_bytes=56 * 1024 * 1024),
        name="scatter",
    )(r4, route_row, gwg, gwu, gwd)
    return (
        gt, gwg[None], gwu[None], jnp.swapaxes(gwd, 0, 1)[None], gg.reshape(gates.shape),
    )


def solution(mesh):
    return jax.shard_map(
        local,
        mesh=mesh,
        in_specs=(
            P(("dp", "expert"), None),
            P(("dp", "expert"), None),
            P("dp", "expert", None, None),
            P("dp", "expert", None, None),
            P("expert", "dp", None),
            P("expert", "dp", None),
            P("expert", None, "dp"),
        ),
        out_specs=(
            P(("dp", "expert"), None),
            P("expert", "dp", None),
            P("expert", "dp", None),
            P("expert", None, "dp"),
            P("dp", "expert", None, None),
        ),
        check_vma=False,
    )
```

```python
import functools

import jax
import jax.numpy as jnp
from jax import lax
from jax.experimental import pallas as pl
from jax.experimental.pallas import tpu as pltpu
from jax.sharding import PartitionSpec as P

NX = 2
F32 = jnp.float32
BF16 = jnp.bfloat16


def dot(a, b, ca=1, cb=0):
    return lax.dot_general(a, b, (((ca,), (cb,)), ((), ())), preferred_element_type=F32)


def one_hot_rows(route, tok_dev):
    n_ex = route.shape[1]
    t_id = lax.broadcasted_iota(jnp.int32, (tok_dev, n_ex), 0)
    return jnp.where(t_id == jnp.broadcast_to(route, (tok_dev, n_ex)), 1.0, 0.0).astype(BF16)


def kernel(
    cfg,
    tokens, grad_out, route, gates, wg, wu, wd,
    r4, gwg_out, gwu_out, gwd_out,
    tok_v, dyo_v, wg_v, wu_v, wd_v, route_v, gates_v, wide, perm, a1, b1, r1, a2, r2, xd,
    part, xa, arm_a, acc_a, arm_b, acc_b, xsend, xrecv, q_all, own_gg, grad_rows, a3, r3, a4, gw_v,
    load_sem, s1_sem, r1_sem, s2_sem, r2_sem, xas_sem, xar_sem, as_sem, ar_sem, xs_sem, xr_sem,
    qs_sem, qr_sem, qxs_sem, qxr_sem, s3_sem, r3_sem, s4_sem, r4_sem, out_sem,
):
    n_dp, n_ex, piece, width, hid = cfg
    ny = n_dp // NX
    n_rows = n_dp * n_ex
    d_model = n_dp * piece
    cap = n_ex
    hh = hid // 2
    win = width + 128
    lanes = width // 2

    me = lax.axis_index("dp")
    ex = lax.axis_index("expert")
    xl = me // ny
    y = lax.rem(me, ny)
    pair = (1 - xl) * ny + y

    def y_of(off):
        return lax.rem(y + off + 2 * ny, ny)

    def y_dev(off):
        return {"dp": xl * ny + y_of(off)}

    def rows(k, n):
        return pl.ds(pl.multiple_of(k * n, n), n)

    barrier = pltpu.get_barrier_semaphore()

    def greet_dp(s, c):
        pl.semaphore_signal(barrier, inc=1, device_id={"dp": lax.rem(me + s, n_dp)})
        return c

    def greet_ex(s, c):
        pl.semaphore_signal(barrier, inc=1, device_id={"expert": lax.rem(ex + s, n_ex)})
        return c

    lax.fori_loop(1, n_ex, greet_ex, 0)
    lax.fori_loop(1, n_dp, greet_dp, 0)

    loads = [
        pltpu.make_async_copy(src, dst, load_sem.at[n])
        for n, (src, dst) in enumerate(
            [
                (route, route_v), (gates, gates_v), (tokens, tok_v), (grad_out, dyo_v),
                (wg, wg_v), (wu, wu_v), (wd, wd_v),
            ]
        )
    ]
    for load in loads:
        load.start()

    lane = lax.broadcasted_iota(jnp.int32, (n_ex, width), 1)
    wide[:, d_model:] = jnp.zeros((n_ex, wide.shape[1] - d_model), F32)
    r_id = lax.broadcasted_iota(jnp.int32, (n_rows, n_rows), 0)
    c_id = lax.broadcasted_iota(jnp.int32, (n_rows, n_rows), 1)
    bits = n_dp.bit_length() - 1
    source = (r_id & (n_dp - 1)) * n_ex + lax.shift_right_logical(r_id, bits)
    perm[...] = jnp.where(c_id == source, 1.0, 0.0).astype(BF16)
    for load in loads[:3]:
        load.wait()
    pick = one_hot_rows(route_v[...], tok_v.shape[0])
    e_row = lax.broadcasted_iota(jnp.int32, (n_ex, n_ex), 0)
    e_col = lax.broadcasted_iota(jnp.int32, (n_ex, n_ex), 1)
    gate_row = jnp.broadcast_to(gates_v[...].astype(F32), (n_ex, n_ex))
    gate_own = jnp.sum(jnp.where(e_row == e_col, gate_row, 0.0), axis=1, keepdims=True)

    def gather(q, src):
        wide[:, :d_model] = dot(pick, src[...], 0, 0)
        for d in range(n_dp):
            start = (piece * d) // 128 * 128
            shift = piece * d - start
            v = wide[:, start:start + win]
            if shift:
                v = pltpu.roll(v, win - shift, 1)
            v = v[:, :width]
            pad = jnp.where(lane == piece, gate_own, 0.0) if q == 0 else 0.0
            v = jnp.where(lane < piece, v, pad).astype(BF16)
            for c in range(2):
                a1[q, c, d * n_ex:(d + 1) * n_ex, :] = v[:, c * lanes:(c + 1) * lanes]

    class Exchange:
        def __init__(self, axis, q, c, src, dst, send, recv):
            self.axis = axis
            self.n, self.mine, self.size = (n_dp, me, n_ex) if axis == "dp" else (n_ex, ex, n_dp)
            self.src, self.dst = src, dst.at[q, c]
            self.send, self.recv = send.at[q, c], recv.at[q, c]

        def start(self):
            own = rows(self.mine, self.size)
            pltpu.make_async_copy(self.src.at[own], self.dst.at[own], self.recv).start()

            def go(s, c):
                k = lax.rem(self.mine + s, self.n)
                pltpu.make_async_remote_copy(
                    src_ref=self.src.at[rows(k, self.size)],
                    dst_ref=self.dst.at[own],
                    send_sem=self.send,
                    recv_sem=self.recv,
                    device_id={self.axis: k},
                ).start()
                return c

            lax.fori_loop(1, self.n, go, 0)

        def arrive(self):
            pltpu.make_async_copy(self.src, self.dst, self.recv).wait()

        def drain(self):
            sent = self.src.at[pl.ds(0, (self.n - 1) * self.size)]
            pltpu.make_async_copy(sent, sent, self.send).wait()

    axes = ("dp", "expert")

    def pair_of(q, first, second, r_first, r_second, sems):
        return (
            [Exchange(axes[c], q, c, first(c), r_first, *sems[:2]) for c in range(2)],
            [Exchange(axes[1 - c], q, c, second(c), r_second, *sems[2:]) for c in range(2)],
        )

    def in_pair(q):
        return pair_of(
            q,
            lambda c: b1.at[q] if c else a1.at[q, 0],
            lambda c: a2.at[q, c],
            r1, r2, (s1_sem, r1_sem, s2_sem, r2_sem),
        )

    ins = [in_pair(q) for q in range(2)]

    def by_expert(v):
        return dot(perm[...], v).astype(BF16)

    def by_dp(v):
        return dot(perm[...], v, 0, 0).astype(BF16)

    for q, src in enumerate((tok_v, dyo_v)):
        if q == 1:
            loads[3].wait()
        gather(q, src)
        if q == 0:
            pl.semaphore_wait(barrier, n_dp + n_ex - 2)
        ins[q][0][0].start()
        b1[q] = by_expert(a1[q, 1])
        ins[q][0][1].start()
    for q in range(2):
        first, second = ins[q]
        first[0].arrive()
        a2[q, 0] = by_expert(r1[q, 0])
        second[0].start()
        first[1].arrive()
        a2[q, 1] = by_dp(r1[q, 1])
        second[1].start()

    def settle(q):
        second = ins[q][1]
        second[0].arrive()
        xd[q, :, :lanes] = r2[q, 0]
        second[1].arrive()
        xd[q, :, lanes:] = by_expert(r2[q, 1])

    for load in loads[4:]:
        load.wait()

    def partial(m, value):
        value = value.astype(BF16)
        for c in range(2):
            part[m, c] = value[:, c * hh:(c + 1) * hh].reshape(NX, ny, cap, hh)

    def arm_len(m, c, s):
        return ny // 2 - (m + c + s) % 2

    def sign(s):
        return 1 - 2 * s

    def xa_copy(m, off):
        block = y_of(off)
        return pltpu.make_async_remote_copy(
            src_ref=part.at[m, 0, 1 - xl, block],
            dst_ref=xa.at[m, block],
            send_sem=xas_sem.at[0],
            recv_sem=xar_sem.at[m, off % ny],
            device_id={"dp": pair},
        )

    def xa_send(m, level):
        long = sign(m % 2)
        n = ny // 2 - level
        for off in {1: (long,), 0: (0,)}.get(n, (n * long, (1 - n) * long)):
            xa_copy(m, off).start()

    def arm_copy(m, c, s, h):
        arm, acc = ((arm_a, acc_a), (arm_b, acc_b))[c]
        if c == 1 and h == 0:
            src = part.at[m, 1, :, y_of(sign(s) * arm_len(m, c, s))]
        else:
            src = acc.at[m, s, h]
        return pltpu.make_async_remote_copy(
            src_ref=src,
            dst_ref=arm.at[m, s, h],
            send_sem=as_sem.at[c],
            recv_sem=ar_sem.at[m, c, s, h],
            device_id=y_dev(sign(s)),
        )

    def hop(m, c, h):
        for s in range(2):
            n = arm_len(m, c, s)
            if h >= n:
                continue
            off = sign(s) * (n - h)
            owner = y_of(off)
            if c == 0:
                xa_copy(m, off).wait_recv()
                v = part[m, 0, xl, owner].astype(F32) + xa[m, owner].astype(F32)
                if h > 0:
                    arm_copy(m, c, s, h - 1).wait_recv()
                    v = v + arm_a[m, s, h - 1].astype(F32)
                acc_a[m, s, h] = v.astype(BF16)
            elif h > 0:
                arm_copy(m, c, s, h - 1).wait_recv()
                v = part[m, 1, :, owner].astype(F32) + arm_b[m, s, h - 1].astype(F32)
                acc_b[m, s, h] = v.astype(BF16)
            arm_copy(m, c, s, h).start()

    def x_copy(m):
        return pltpu.make_async_remote_copy(
            src_ref=xsend.at[m],
            dst_ref=xrecv.at[m],
            send_sem=xs_sem.at[0],
            recv_sem=xr_sem.at[m],
            device_id={"dp": pair},
        )

    def b_total(m, side):
        v = part[m, 1, side, y].astype(F32)
        for s in range(2):
            v = v + arm_b[m, s, arm_len(m, 1, s) - 1, side].astype(F32)
        return v

    def b_end(m):
        for s in range(2):
            arm_copy(m, 1, s, arm_len(m, 1, s) - 1).wait_recv()
        xsend[m] = b_total(m, 1 - xl).astype(BF16)
        x_copy(m).start()

    def end_a(m):
        xa_copy(m, 0).wait_recv()
        v = part[m, 0, xl, y].astype(F32) + xa[m, y].astype(F32)
        for s in range(2):
            n = arm_len(m, 0, s)
            arm_copy(m, 0, s, n - 1).wait_recv()
            v = v + arm_a[m, s, n - 1].astype(F32)
        return v

    def end_b(m):
        x_copy(m).wait_recv()
        return b_total(m, xl) + xrecv[m].astype(F32)

    last = ny // 2

    settle(0)
    partial(0, dot(xd[0, :, :piece], wg_v[...]))
    hop(0, 1, 0)
    xa_send(0, 0)
    partial(1, dot(xd[0, :, :piece], wu_v[...]))
    hop(1, 1, 0)
    xa_send(1, 0)
    xa_send(0, 1)
    xa_send(1, 1)
    settle(1)
    partial(2, dot(xd[1, :, :piece], wd_v[...]))
    hop(2, 1, 0)
    xa_send(2, 0)
    xa_send(2, 1)
    for level in range(2, last + 1):
        for m in range(3):
            xa_send(m, level)
    for h in range(1, last + 1):
        for m in range(3):
            if h < last:
                hop(m, 1, h)
            elif h == last:
                b_end(m)
        if h >= 1:
            for m in range(3):
                hop(m, 0, h - 1)

    gate_rows = xd[0, rows(me, cap), :].astype(F32)
    wl = lax.broadcasted_iota(jnp.int32, (cap, width), 1)
    gate_w = jnp.sum(jnp.where(wl == piece, gate_rows, 0.0), axis=1, keepdims=True)

    def activate(c, end):
        gate_pre = end(0)
        up_pre = end(1)
        sig = 1.0 / (1.0 + jnp.exp(-gate_pre))
        act = gate_pre * sig
        hidden = act * up_pre
        slope = up_pre * sig * (1.0 + gate_pre * (1.0 - sig))
        base = end(2)
        grad_hidden = gate_w * base
        q_all[1, c, xl, y] = (grad_hidden * slope).astype(BF16)
        q_all[2, c, xl, y] = (grad_hidden * act).astype(BF16)
        q_all[0, c, xl, y] = (gate_w * hidden).astype(BF16)
        return jnp.sum(hidden * base, axis=1, keepdims=True)

    def q_remote(block, send, recv, device):
        return pltpu.make_async_remote_copy(
            src_ref=block, dst_ref=block, send_sem=send, recv_sem=recv, device_id=device
        )

    def q_xb(m):
        return q_remote(q_all.at[m, 1, xl, y], qxs_sem.at[1], qxr_sem.at[m, 1], {"dp": pair})

    def q_xa(m, off):
        block = q_all.at[m, 0, xl, y_of(off)]
        return q_remote(block, qxs_sem.at[0], qxr_sem.at[m, 0], {"dp": pair})

    def q_arm(m, c, s, h):
        owner = y_of(-sign(s) * h)
        block = q_all.at[m, 0, xl, owner] if c == 0 else q_all.at[m, 1, :, owner]
        return q_remote(block, qs_sem.at[c], qr_sem.at[m, c, s, h], y_dev(sign(s)))

    def q_hop(m, c, h):
        if h == 0:
            if c == 0:
                q_xa(m, 0).start()
            else:
                q_xb(m).wait_recv()
        for s in range(2):
            n = arm_len(m, c, s)
            if h > n:
                continue
            if h > 0:
                q_arm(m, c, s, h - 1).wait_recv()
            if h < n:
                q_arm(m, c, s, h).start()
            if c == 0 and h > 0:
                q_xa(m, -sign(s) * h).start()

    def q_end(m):
        side = q_all.at[m, 0, 1 - xl]
        pltpu.make_async_copy(side, side, qxr_sem.at[m, 0]).wait()

    gg = activate(1, end_b)
    for m in (1, 2, 0):
        q_xb(m).start()
    gg = gg + activate(0, end_a)
    own_gg[...] = jnp.broadcast_to(gg, own_gg.shape)
    for m in (1, 2):
        q_hop(m, 1, 0)
        q_hop(m, 0, 0)
    for h in range(1, last + 1):
        for m, k in ((1, h), (2, h), (0, h - 2)):
            if m > 0 or 0 <= k < last - 2:
                q_hop(m, 0, k)
                q_hop(m, 1, k)
    q_end(1)

    def back(m):
        return jnp.concatenate(
            [q_all[m, c].reshape(n_rows, hh) for c in range(2)], axis=1
        )

    def rows_grad(m, w, lo, hi):
        return dot(back(m), w[lo:hi, :], 1, 1)

    home = [
        Exchange("expert", 0, 0, a3.at[0], r3, s3_sem, r3_sem),
        Exchange("dp", 0, 1, a3.at[1], r3, s3_sem, r3_sem),
    ]
    home2 = [
        Exchange("dp", 0, 0, a4.at[0], r4, s4_sem, r4_sem),
        Exchange("expert", 0, 1, a4.at[1], r4, s4_sem, r4_sem),
    ]
    gate_part = rows_grad(1, wg_v, 0, lanes)
    q_end(2)
    a3[0] = (gate_part + rows_grad(2, wu_v, 0, lanes)).astype(BF16)
    home[0].start()
    grad_rows[...] = jnp.zeros((n_rows, lanes), BF16)
    grad_rows[:, :piece - lanes] = (
        rows_grad(1, wg_v, lanes, piece) + rows_grad(2, wu_v, lanes, piece)
    ).astype(BF16)
    tail = grad_rows[rows(me, cap), :].astype(F32)
    tl = lax.broadcasted_iota(jnp.int32, tail.shape, 1) + lanes
    rest = own_gg[...]
    for n in range(3):
        top = rest.astype(BF16).astype(F32)
        tail = jnp.where(tl == piece + n, top, tail)
        rest = rest - top
    grad_rows[rows(me, cap), :] = tail.astype(BF16)

    a3[1] = by_dp(grad_rows[...])
    home[1].start()

    outs = [
        pltpu.make_async_copy(gw_v.at[m], dst, out_sem.at[m])
        for m, dst in ((1, gwg_out), (2, gwu_out), (0, gwd_out))
    ]
    q_hop(0, 1, last - 2)
    q_hop(0, 0, last - 2)
    gw_v[1] = dot(xd[0, :, :piece], back(1), 0, 0).astype(BF16)
    outs[0].start()
    q_hop(0, 1, last - 1)
    q_hop(0, 0, last - 1)
    gw_v[2] = dot(xd[0, :, :piece], back(2), 0, 0).astype(BF16)
    outs[1].start()
    home[0].arrive()
    a4[0] = by_dp(r3[0, 0])
    home2[0].start()
    home[1].arrive()
    a4[1] = by_expert(r3[0, 1])
    home2[1].start()
    q_hop(0, 1, last)
    q_hop(0, 0, last)
    q_end(0)
    gw_v[0] = dot(xd[1, :, :piece], back(0), 0, 0).astype(BF16)
    outs[2].start()
    for x in home2:
        x.arrive()

    for x in (*ins[0][0], *ins[0][1], *ins[1][0], *ins[1][1], *home, *home2):
        x.drain()

    def sent(ref, sem):
        pltpu.make_async_copy(ref, ref, sem).wait()

    sent(part.at[:, 0, 0], xas_sem.at[0])
    sent(part.at[:, 0, 0, pl.ds(0, ny - 1)], as_sem.at[0])
    sent(part.at[:, 1, :, pl.ds(0, ny - 1)], as_sem.at[1])
    sent(xsend, xs_sem.at[0])
    sent(part.at[:, 0, 0], qxs_sem.at[0])
    sent(xsend, qxs_sem.at[1])
    sent(part.at[:, 0, 0, pl.ds(0, ny - 1)], qs_sem.at[0])
    sent(part.at[:, 1, :, pl.ds(0, ny - 1)], qs_sem.at[1])
    for out in outs:
        out.wait()


def last_kernel(
    cfg, r4, route, gwg, gwu, gwd, gt_out, gg_out, gwg_out, gwu_out, gwd_out,
    r4_v, late, route_v, gw_v, wide, gt_v, gg_v, in_sem, out_sem,
):
    n_dp, n_ex, piece, width, hid = cfg
    d_model = n_dp * piece
    win = width + 128
    step = d_model // 4
    parts = [pl.ds(n * step, step) for n in range(4)]
    ins = [
        pltpu.make_async_copy(src, dst, in_sem.at[n])
        for n, (src, dst) in enumerate(
            [(r4, r4_v), (route, route_v)]
            + [(src, gw_v.at[m]) for m, src in enumerate((gwg, gwu, gwd))]
        )
    ]
    outs = [
        pltpu.make_async_copy(src, dst, out_sem.at[n])
        for n, (src, dst) in enumerate(
            [(gw_v.at[m], dst) for m, dst in enumerate((gwg_out, gwu_out, gwd_out))]
            + [(gg_v, gg_out)]
            + [(gt_v.at[:, part], gt_out.at[:, part]) for part in parts]
        )
    ]
    for copy in ins:
        copy.start()
    wide[...] = jnp.zeros(wide.shape, F32)
    ins[0].wait()
    ins[1].wait()
    late[...] = r4_v[0, 1].astype(F32)
    lane = lax.broadcasted_iota(jnp.int32, (n_ex, width), 1)
    sums = jnp.zeros((n_ex, width), F32)
    for d in range(n_dp):
        start = (piece * d) // 128 * 128
        shift = piece * d - start
        v = jnp.concatenate(
            [
                r4_v[0, 0, d * n_ex:(d + 1) * n_ex, :].astype(F32),
                late[pl.ds(d, n_ex, stride=n_dp), :],
            ],
            axis=1,
        )
        sums = sums + jnp.where((lane >= piece) & (lane < piece + 3), v, 0.0)
        v = jnp.concatenate([jnp.where(lane < piece, v, 0.0), jnp.zeros((n_ex, 128), F32)], axis=1)
        if shift:
            v = pltpu.roll(v, shift, 1)
        wide[:, start:start + win] += v
    for n in range(3):
        ins[2 + n].wait()
        outs[n].start()
    e_row = lax.broadcasted_iota(jnp.int32, (n_ex, n_ex), 0)
    e_col = lax.broadcasted_iota(jnp.int32, (n_ex, n_ex), 1)
    column = jnp.broadcast_to(jnp.sum(sums, axis=1, keepdims=True), (n_ex, n_ex))
    gg_v[...] = jnp.sum(jnp.where(e_row == e_col, column, 0.0), axis=0, keepdims=True)
    outs[3].start()
    pick = one_hot_rows(route_v[...], gt_v.shape[0])
    for n in range(4):
        cut = slice(n * step, (n + 1) * step)
        gt_v[:, cut] = dot(pick, wide[:, cut].astype(BF16)).astype(BF16)
        outs[4 + n].start()
    for copy in outs:
        copy.wait()


def local(tokens, grad_out, route, gates, w_gate, w_up, w_down):
    n_dp = lax.axis_size("dp")
    n_ex = lax.axis_size("expert")
    piece, hid = w_gate.shape[1:]
    tok_dev, d_model = tokens.shape
    width = (piece + 3 + 127) // 128 * 128
    n_rows = n_dp * n_ex
    ny = n_dp // NX
    hops = ny // 2
    cap = n_ex
    hh = hid // 2
    dma = pltpu.SemaphoreType.DMA
    any_spec = pl.BlockSpec(memory_space=pl.ANY)
    cfg = (n_dp, n_ex, piece, width, hid)
    weights = jax.ShapeDtypeStruct((piece, hid), BF16)
    route_row = route.reshape(1, n_ex)
    wide = pltpu.VMEM((n_ex, d_model + width + 128), F32)
    lanes = width // 2
    whole = pltpu.VMEM((2, n_rows, width), BF16)
    block = pltpu.VMEM((2, 2, n_rows, lanes), BF16)
    halves = pltpu.VMEM((2, n_rows, lanes), BF16)
    r4, gwg, gwu, gwd = pl.pallas_call(
        functools.partial(kernel, cfg),
        out_shape=(jax.ShapeDtypeStruct((1, 2, n_rows, lanes), BF16), weights, weights, weights),
        in_specs=[any_spec] * 7,
        out_specs=(any_spec,) * 4,
        scratch_shapes=[
            pltpu.VMEM((tok_dev, d_model), BF16),
            pltpu.VMEM((tok_dev, d_model), BF16),
            pltpu.VMEM((piece, hid), BF16),
            pltpu.VMEM((piece, hid), BF16),
            pltpu.VMEM((piece, hid), BF16),
            pltpu.VMEM((1, n_ex), jnp.int32),
            pltpu.VMEM((1, n_ex), BF16),
            wide,
            pltpu.VMEM((n_rows, n_rows), BF16),
            block, halves, block, block, block, whole,
            pltpu.VMEM((3, 2, NX, ny, cap, hh), BF16),
            pltpu.VMEM((3, ny, cap, hh), BF16),
            pltpu.VMEM((3, 2, hops, cap, hh), BF16),
            pltpu.VMEM((3, 2, hops, cap, hh), BF16),
            pltpu.VMEM((3, 2, hops, NX, cap, hh), BF16),
            pltpu.VMEM((3, 2, hops, NX, cap, hh), BF16),
            pltpu.VMEM((3, cap, hh), BF16),
            pltpu.VMEM((3, cap, hh), BF16),
            pltpu.VMEM((3, 2, NX, ny, cap, hh), BF16),
            pltpu.VMEM((cap, 128), F32),
            pltpu.VMEM((n_rows, lanes), BF16),
            halves,
            pltpu.VMEM((1, 2, n_rows, lanes), BF16),
            halves,
            pltpu.VMEM((3, piece, hid), BF16),
            dma((7,)),
            dma((2, 2)), dma((2, 2)),
            dma((2, 2)), dma((2, 2)),
            dma((1,)), dma((3, ny)),
            dma((2,)), dma((3, 2, 2, hops)),
            dma((1,)), dma((3,)),
            dma((2,)), dma((3, 2, 2, hops)),
            dma((2,)), dma((3, 2)),
            dma((1, 2)), dma((1, 2)),
            dma((1, 2)), dma((1, 2)),
            dma((3,)),
        ],
        compiler_params=pltpu.CompilerParams(
            collective_id=0, has_side_effects=True, vmem_limit_bytes=56 * 1024 * 1024
        ),
        name="moe",
    )(
        tokens,
        grad_out,
        route_row,
        gates.reshape(1, n_ex),
        w_gate[0],
        w_up[0],
        jnp.swapaxes(w_down[0], 0, 1),
    )
    gt, gg, gwg, gwu, gwd = pl.pallas_call(
        functools.partial(last_kernel, cfg),
        out_shape=(
            jax.ShapeDtypeStruct((tok_dev, d_model), BF16),
            jax.ShapeDtypeStruct((1, n_ex), F32),
            weights, weights, weights,
        ),
        in_specs=[any_spec] * 5,
        out_specs=(any_spec,) * 5,
        scratch_shapes=[
            pltpu.VMEM((1, 2, n_rows, lanes), BF16),
            pltpu.VMEM((n_rows, lanes), F32),
            pltpu.VMEM((1, n_ex), jnp.int32),
            pltpu.VMEM((3, piece, hid), BF16),
            wide,
            pltpu.VMEM((tok_dev, d_model), BF16),
            pltpu.VMEM((1, n_ex), F32),
            dma((5,)),
            dma((8,)),
        ],
        compiler_params=pltpu.CompilerParams(vmem_limit_bytes=56 * 1024 * 1024),
        name="scatter",
    )(r4, route_row, gwg, gwu, gwd)
    return (
        gt, gwg[None], gwu[None], jnp.swapaxes(gwd, 0, 1)[None], gg.reshape(gates.shape),
    )


def solution(mesh):
    return jax.shard_map(
        local,
        mesh=mesh,
        in_specs=(
            P(("dp", "expert"), None),
            P(("dp", "expert"), None),
            P("dp", "expert", None, None),
            P("dp", "expert", None, None),
            P("expert", "dp", None),
            P("expert", "dp", None),
            P("expert", None, "dp"),
        ),
        out_specs=(
            P(("dp", "expert"), None),
            P("expert", "dp", None),
            P("expert", "dp", None),
            P("expert", None, "dp"),
            P("dp", "expert", None, None),
        ),
        check_vma=False,
    )
```
